256 devices in a mesh: grp: 8 (over y, core), dev: 32 (over z, x).
Axes of the slice: x: 4, y: 4, z: 8, core: 2. Of those that a mesh axis runs over, the one named last changes fastest.
Arguments:
- u_blocks: float32 [6144, 32, 1024], P(('grp', 'dev')), may hold values from -20 to 20
- v_blocks: float32 [6144, 32, 1024], P(('grp', 'dev')), may hold values from -0.1875 to 0.1875
- sketch: float32 [512, 32, 1024], P(('grp', 'dev')), may hold values from -6 to 6
- near_diag: float32 [512, 1024], P(('grp', 'dev')), may hold values from 0.3 to 72
- block_row: int32 [6144], P(('grp', 'dev')), may hold values from 0 to 63, as said below
- col_count: int32 [512], P(('grp', 'dev')), may hold values from 8 to 12, as said below
Outputs:
- leaf_basis: float32 [512, 32, 1024], P(('grp', 'dev'))
- transfer_leaf: float32 [512, 32, 32], P(('grp', 'dev'))
- transfer_group: float32 [8, 32, 32], P('grp')
The draws below stay inside these ranges and needn't reach their ends.
Inputs may be any that keep to these rules, and one draw needn't show every extreme that they name: A device's slots hold its blocks in the order of its column clusters, col_count[c] of them for cluster c; the remaining slots are empty. The row cluster block_row[s] belongs to device block_row[s] // 2 of the same subtree. Among the live slots of one device at most 3 have row clusters of any one device, and in every subtree some device is named by exactly 3 live slots of every device of that subtree.
All inputs are finite; a program needn't handle non-finite values.
Results may differ from the reference program's by a relative error of at most 0.0003.
Values sent between devices are 32-bit elements; how exact they have to be, the bound alone decides.
No kernel may reach another device: no remote copies, remote signals or barrier semaphores. Data moves between devices by JAX's collectives and lax.ppermute only.
A program may use at most 128 MiB of HBM per device.

```python
import math
import jax
import jax.numpy as jnp
from jax import lax

R = 32
LEAF = 1024
L_DEV = 2
CMIN = 8
CMAX = 12
MEMBERS = 32
GROUPS = 8
CAP = 3
BLK_DEV = 24
CLUSTERS = 512
NBLK = 6144


def route_plan(key):
    base_key = jax.random.fold_in(key, 4242)
    key_count, key_busy, key_pool, key_front, key_local = jax.random.split(base_key, 5)
    devices_all = GROUPS * MEMBERS
    counts = jax.random.randint(key_count, (devices_all * L_DEV,), CMIN, CMAX + 1).astype(jnp.int32)
    busy_group = jax.random.randint(key_busy, (GROUPS,), 0, MEMBERS).astype(jnp.int32)
    busy_dev = jnp.repeat(busy_group, MEMBERS)
    others = (busy_dev[:, None] + 1 + jnp.arange(MEMBERS - 1, dtype=jnp.int32)[None, :]) % MEMBERS
    spread = jnp.repeat(others, CAP, axis=1)
    pool_keys = jax.random.split(key_pool, devices_all)
    shuffled = jax.vmap(jax.random.permutation)(pool_keys, spread)
    pool = jnp.concatenate([jnp.repeat(busy_dev[:, None], CAP, axis=1), shuffled], axis=1)[:, :BLK_DEV]
    front_len = L_DEV * CMIN
    front_keys = jax.random.split(key_front, devices_all)
    front_order = jax.vmap(lambda key_one: jax.random.permutation(key_one, front_len))(front_keys)
    head_part = jnp.take_along_axis(pool[:, :front_len], front_order, axis=1)
    pool = jnp.concatenate([head_part, pool[:, front_len:]], axis=1)
    local_ids = jax.random.randint(key_local, (devices_all, BLK_DEV), 0, L_DEV).astype(jnp.int32)
    row_ids = (pool * L_DEV + local_ids).astype(jnp.int32)
    return (counts, row_ids.reshape(-1))


def rise_of(owner_dev, group_ids):
    return (1.0 + 2.0 * owner_dev / max(MEMBERS - 1, 1)) * (1.0 + 2.0 * group_ids / max(GROUPS - 1, 1))


def draw_block_row(key, part):
    return route_plan(key)[1]


def draw_col_count(key, part):
    return route_plan(key)[0]


def draw_u_blocks(key, part):
    counts, row_ids = route_plan(key)
    block_total = GROUPS * MEMBERS * BLK_DEV
    key_entries, key_scale = jax.random.split(jax.random.fold_in(key, 99))
    owner_dev = (row_ids // L_DEV).astype(jnp.float32)
    group_ids = (jnp.arange(block_total) // (BLK_DEV * MEMBERS)).astype(jnp.float32)
    rise_factor = rise_of(owner_dev, group_ids)
    entries = jax.random.truncated_normal(key_entries, -4.0, 4.0, (block_total, R, LEAF), jnp.float32)
    block_scale = jnp.exp(jax.random.uniform(key_scale, (block_total,), jnp.float32, math.log(0.5), math.log(2.0)))
    return entries * (rise_factor * block_scale)[:, None, None] / math.sqrt(R)


def draw_near_diag(key, part):
    key_values = jax.random.fold_in(key, 77)
    cluster_ids = jnp.arange(CLUSTERS)
    group_ids = (cluster_ids // (MEMBERS * L_DEV)).astype(jnp.float32)
    owner_dev = (cluster_ids % (MEMBERS * L_DEV) // L_DEV).astype(jnp.float32)
    rise_factor = rise_of(owner_dev, group_ids)
    values = jnp.exp(jax.random.uniform(key_values, (CLUSTERS, LEAF), jnp.float32, math.log(0.5), math.log(5.0)))
    return values * rise_factor[:, None]


def level_of(key, extent, shards, low, high):
    loudness, own = 1.0, jax.random.fold_in(key, 6)
    for position, parts in shards:
        steps = jnp.exp(jax.random.uniform(jax.random.fold_in(own, position), (parts,), jnp.float32, low / len(shards), high / len(shards)))
        loudness = loudness * jnp.repeat(steps, extent[position] // parts).reshape([-1 if axis == position else 1 for axis in range(len(extent))])
    return loudness


def noise(own_key, dims, deviation, reach, shards=(), kind=jnp.bfloat16):
    loudness = level_of(own_key, dims, shards, -0.22, 0.18) if shards else 1.0
    drawn = jax.random.normal(own_key, dims, jnp.float32) * deviation * loudness
    return jnp.minimum(jnp.maximum(drawn, -reach), reach).astype(kind)


def setup_inputs(seed: int = 0) -> dict:
    key_list = jax.random.split(jax.random.key(seed), 7)
    return {
        "u_blocks": draw_u_blocks(jax.random.fold_in(key_list[6], 71), 0),
        "v_blocks": noise(key_list[1], (NBLK, R, LEAF), LEAF ** -0.5, 0.1875, ((0, 256),), jnp.float32),
        "sketch": noise(key_list[2], (CLUSTERS, R, LEAF), 1.0, 6.0, ((0, 256),), jnp.float32),
        "near_diag": draw_near_diag(jax.random.fold_in(key_list[6], 71), 0),
        "block_row": draw_block_row(jax.random.fold_in(key_list[6], 71), 0),
        "col_count": draw_col_count(jax.random.fold_in(key_list[6], 71), 0),
    }


def positive_qr(stacked):
    q_factor, r_factor = jnp.linalg.qr(stacked)
    sign_flip = jnp.sign(jnp.diagonal(r_factor, axis1=-2, axis2=-1))
    return (q_factor * sign_flip[..., None, :], r_factor * sign_flip[..., :, None])

def reference(u_blocks, v_blocks, sketch, near_diag, block_row, col_count):
    highest = lax.Precision.HIGHEST
    devices_all = GROUPS * MEMBERS
    counts = col_count.reshape(devices_all, L_DEV)
    slot_ends = jnp.cumsum(counts, axis=1)
    slot_index = jnp.arange(BLK_DEV, dtype=jnp.int32)
    alive_slot = slot_index[None, :] < slot_ends[:, -1:]
    col_local = jnp.minimum(lax.optimization_barrier(jnp.sum((slot_ends[:, None, :] <= slot_index[None, :, None]).astype(jnp.int32), axis=2)), L_DEV - 1)
    device_ids = jnp.arange(devices_all, dtype=jnp.int32)[:, None]
    col_ids = (device_ids * L_DEV + col_local).astype(jnp.int32)
    row_ids = (device_ids // MEMBERS * (MEMBERS * L_DEV) + block_row.reshape(devices_all, BLK_DEV)).astype(jnp.int32)

    def accumulate(running, pieces):
        u_part, v_part, col_part, row_part, alive_part = pieces
        picked = sketch[col_part]
        coupling = jnp.einsum('bkl,bml->bkm', v_part, picked, precision=highest)
        coupling = jnp.where(alive_part[:, None, None], coupling, 0.0)
        contribution = jnp.einsum('bkm,bkl->bml', coupling, u_part, precision=highest)
        return (running.at[row_part].add(contribution), None)
    initial = jnp.zeros(sketch.shape, jnp.float32)
    far_sample, _ = lax.scan(accumulate, initial, (u_blocks.reshape(devices_all, BLK_DEV, R, LEAF), v_blocks.reshape(devices_all, BLK_DEV, R, LEAF), col_ids, row_ids, alive_slot))
    sample = far_sample + near_diag[:, None, :] * sketch
    q_leaf, r_leaf = positive_qr(jnp.swapaxes(sample, 1, 2))
    leaf_basis = jnp.swapaxes(q_leaf, 1, 2) * math.sqrt(LEAF)
    q_group, r_group = positive_qr(r_leaf.reshape(GROUPS, MEMBERS * L_DEV * R, R))
    transfer_leaf = q_group.reshape(CLUSTERS, R, R) * math.sqrt(MEMBERS * L_DEV)
    q_root, r_root = positive_qr(r_group.reshape(GROUPS * R, R))
    transfer_group = q_root.reshape(GROUPS, R, R) * math.sqrt(GROUPS)
    return (leaf_basis, transfer_leaf, transfer_group)
```

```python
import functools
import math

import jax
import jax.numpy as jnp
from jax import lax
from jax.experimental import pallas as pl
from jax.experimental.pallas import tpu as pltpu
from jax.sharding import PartitionSpec as P

NZ, NX = 8, 4
R = 32
LEAF = 1024
SPLIT = 512
SLOTS_STEP = 4
HIGHEST = lax.Precision.HIGHEST


def halves(value):
    high = value.astype(jnp.bfloat16)
    low = (value - high.astype(jnp.float32)).astype(jnp.bfloat16)
    return high, low


def contribution_kernel(rows_ref, count_ref, place_ref, u_ref, v_ref, sketch_ref, xfirst_ref, zfirst_ref):
    step = pl.program_id(0)

    @pl.when(step == 0)
    def _():
        xfirst_ref[...] = jnp.zeros_like(xfirst_ref)
        zfirst_ref[...] = jnp.zeros_like(zfirst_ref)

    first_count = count_ref[0]
    live_count = first_count + count_ref[1]
    sketch_high, sketch_low = halves(sketch_ref[...].reshape(2 * R, LEAF))
    v_high, v_low = halves(v_ref[...].reshape(SLOTS_STEP * R, LEAF))
    contract = (((1,), (1,)), ((), ()))
    both = jnp.concatenate([sketch_high, sketch_low], axis=0)
    wide = lax.dot_general(v_high, both, contract, preferred_element_type=jnp.float32)
    couplings = (
        wide[:, : 2 * R]
        + wide[:, 2 * R :]
        + lax.dot_general(v_low, sketch_high, contract, preferred_element_type=jnp.float32)
    )
    for t in range(SLOTS_STEP):
        slot = step * SLOTS_STEP + t

        @pl.when(slot < live_count)
        def _():
            row = rows_ref[slot]
            device = row // 2
            cluster = row % 2
            dz = (device // NX - place_ref[0] + NZ) % NZ
            dx = (device % NX - place_ref[1] + NX) % NX
            part = couplings[t * R : (t + 1) * R]
            coupling = jnp.where(slot < first_count, part[:, :R], part[:, R:])
            c_high, c_low = halves(coupling)
            u_high, u_low = halves(u_ref[t])
            left = jnp.concatenate([c_high, c_low, c_high], axis=0)
            right = jnp.concatenate([u_high, u_high, u_low], axis=0)
            value = lax.dot_general(
                left, right, (((0,), (0,)), ((), ())), preferred_element_type=jnp.float32
            )
            xfirst_ref[dx, cluster, dz] += value[:, :SPLIT]
            zfirst_ref[dz, cluster, dx] += value[:, SPLIT:]


def contributions(block_row, col_count, place, u_blocks, v_blocks, sketch):
    slots = u_blocks.shape[0]
    xshape = (NX, 2, NZ, R, SPLIT)
    zshape = (NZ, 2, NX, R, LEAF - SPLIT)
    block = lambda i, *_: (i, 0, 0)
    whole = lambda i, *_: (0, 0, 0, 0, 0)
    return pl.pallas_call(
        contribution_kernel,
        out_shape=(
            jax.ShapeDtypeStruct(xshape, jnp.float32),
            jax.ShapeDtypeStruct(zshape, jnp.float32),
        ),
        grid_spec=pltpu.PrefetchScalarGridSpec(
            num_scalar_prefetch=3,
            grid=(slots // SLOTS_STEP,),
            in_specs=[
                pl.BlockSpec((SLOTS_STEP, R, LEAF), block),
                pl.BlockSpec((SLOTS_STEP, R, LEAF), block),
                pl.BlockSpec((2, R, LEAF), lambda i, *_: (0, 0, 0)),
            ],
            out_specs=(pl.BlockSpec(xshape, whole), pl.BlockSpec(zshape, whole)),
        ),
        compiler_params=pltpu.CompilerParams(vmem_limit_bytes=40 << 20),
        cost_estimate=pl.CostEstimate(flops=10**9, bytes_accessed=16 << 20, transcendentals=0),
        name="contributions",
    )(block_row, col_count, place, u_blocks, v_blocks, sketch)


def shift(value, dz, dx):
    pairs = [
        (z * NX + x, (z + dz) % NZ * NX + (x + dx) % NX) for z in range(NZ) for x in range(NX)
    ]
    return lax.ppermute(value, "dev", pairs)


def ring_sum(chunks, plus, minus):
    count = len(chunks)
    middle = count // 2
    forward = plus(chunks[middle][:1])
    backward = minus(chunks[middle][1:])
    for r in range(middle - 1, 0, -1):
        ahead, behind = chunks[r], chunks[count - r]
        if r == middle - 1:
            forward = jnp.concatenate([ahead[:1] + forward, ahead[1:]], axis=0)
            backward = jnp.concatenate([behind[:1], behind[1:] + backward], axis=0)
        else:
            forward = ahead + forward
            backward = behind + backward
        forward = plus(forward)
        backward = minus(backward)
    return chunks[0], forward, backward


def pack(gram):
    return jnp.concatenate([gram[8 * i : 8 * i + 8] for i in range(4)], axis=1)


def unpack(packed):
    return jnp.concatenate([packed[:, R * i : R * i + R] for i in range(4)], axis=0)


def eliminate(grams):
    count = len(grams)
    eye = (
        lax.broadcasted_iota(jnp.int32, (R, R), 0) == lax.broadcasted_iota(jnp.int32, (R, R), 1)
    ).astype(jnp.float32)
    work = [jnp.concatenate([gram, eye], axis=1) for gram in grams]
    sublane = lax.broadcasted_iota(jnp.int32, (R, 2 * R), 0)
    done = [jnp.zeros((R, 2 * R), jnp.float32) for _ in grams]
    for j in range(R):
        for i in range(count):
            column = jnp.broadcast_to(work[i][:, j : j + 1], (R, 2 * R))
            pivot = column[j : j + 1]
            scale = lax.rsqrt(pivot)
            scale = scale * (1.5 - 0.5 * pivot * scale * scale)
            row = jnp.broadcast_to(work[i][j : j + 1] * scale, (R, 2 * R))
            done[i] = jnp.where(sublane == j, row, done[i])
            work[i] = work[i] - (column * jnp.broadcast_to(scale, (R, 2 * R))) * row
    return [(d[:, :R], d[:, R:]) for d in done]


def sample_kernel(xo_ref, xf_ref, xb_ref, zo_ref, zf_ref, zb_ref, diag_ref, sketch_ref, sample_ref, gram_ref, packed_ref):
    total = jnp.zeros((R, R), jnp.float32)
    for i in range(2):
        far = jnp.concatenate(
            [xo_ref[i] + xf_ref[i] + xb_ref[i], zo_ref[i] + zf_ref[i] + zb_ref[i]], axis=1
        )
        sample = far + diag_ref[i : i + 1] * sketch_ref[i]
        sample_ref[i] = sample
        gram = lax.dot_general(
            sample,
            sample,
            (((1,), (1,)), ((), ())),
            precision=HIGHEST,
            preferred_element_type=jnp.float32,
        )
        gram_ref[i] = gram
        total = total + gram
    packed_ref[...] = jnp.broadcast_to(pack(total)[None], packed_ref.shape)


def leaf_kernel(gram_ref, sample_ref, basis_ref, upper_ref):
    factors = eliminate([gram_ref[0], gram_ref[1]])
    for i, (upper, inverse) in enumerate(factors):
        rows = lax.broadcasted_iota(jnp.int32, (R, R), 0)
        cols = lax.broadcasted_iota(jnp.int32, (R, R), 1)
        upper_ref[i] = jnp.where(rows <= cols, upper, 0.0)
        basis_ref[i] = jnp.dot(
            inverse * math.sqrt(LEAF),
            sample_ref[i],
            precision=HIGHEST,
            preferred_element_type=jnp.float32,
        )


def group_kernel(every_ref, packed_ref):
    packed_ref[...] = jnp.broadcast_to(jnp.sum(every_ref[...], axis=0)[None], packed_ref.shape)


def transfer_kernel(leaves, own_ref, every_ref, upper_ref, leaf_ref, group_ref):
    groups = every_ref.shape[0]
    group_gram = unpack(own_ref[0])
    root_gram = unpack(jnp.sum(every_ref[...], axis=0))
    (group_upper, group_inverse), (_, root_inverse) = eliminate([group_gram, root_gram])
    rows = lax.broadcasted_iota(jnp.int32, (R, R), 0)
    cols = lax.broadcasted_iota(jnp.int32, (R, R), 1)
    group_upper = jnp.where(rows <= cols, group_upper, 0.0)
    contract = (((1,), (1,)), ((), ()))
    for i in range(2):
        leaf_ref[i] = lax.dot_general(
            upper_ref[i],
            group_inverse * math.sqrt(leaves),
            contract,
            precision=HIGHEST,
            preferred_element_type=jnp.float32,
        )
    group_ref[0] = lax.dot_general(
        group_upper,
        root_inverse * math.sqrt(groups),
        contract,
        precision=HIGHEST,
        preferred_element_type=jnp.float32,
    )


def body(u_blocks, v_blocks, sketch, near_diag, block_row, col_count):
    members = lax.axis_size("dev")
    groups = lax.axis_size("grp")
    me = lax.axis_index("dev")
    place = jnp.stack([me // NX, me % NX]).astype(jnp.int32)
    xfirst, zfirst = contributions(block_row, col_count, place, u_blocks, v_blocks, sketch)
    along = {
        "x": (lambda a: shift(a, 0, 1), lambda a: shift(a, 0, -1)),
        "z": (lambda a: shift(a, 1, 0), lambda a: shift(a, -1, 0)),
    }
    own, ahead, behind = ring_sum([xfirst[i] for i in range(NX)], *along["x"])
    part = own + ahead + behind
    xterms = ring_sum([part[:, i] for i in range(NZ)], *along["z"])
    own, ahead, behind = ring_sum([zfirst[i] for i in range(NZ)], *along["z"])
    part = own + ahead + behind
    zterms = ring_sum([part[:, i] for i in range(NX)], *along["x"])
    sample, gram, packed = pl.pallas_call(
        sample_kernel,
        out_shape=(
            jax.ShapeDtypeStruct((2, R, LEAF), jnp.float32),
            jax.ShapeDtypeStruct((2, R, R), jnp.float32),
            jax.ShapeDtypeStruct((members, 8, 128), jnp.float32),
        ),
        name="sample",
    )(*xterms, *zterms, near_diag, sketch)
    every = lax.all_to_all(packed, "dev", split_axis=0, concat_axis=0, tiled=True)
    leaf_basis, upper = pl.pallas_call(
        leaf_kernel,
        out_shape=(
            jax.ShapeDtypeStruct((2, R, LEAF), jnp.float32),
            jax.ShapeDtypeStruct((2, R, R), jnp.float32),
        ),
        name="leaf",
    )(gram, sample)
    own_gram = pl.pallas_call(
        group_kernel,
        out_shape=jax.ShapeDtypeStruct((groups, 8, 128), jnp.float32),
        name="group",
    )(every)
    every_group = lax.all_to_all(own_gram, "grp", split_axis=0, concat_axis=0, tiled=True)
    transfer_leaf, transfer_group = pl.pallas_call(
        functools.partial(transfer_kernel, 2 * members),
        out_shape=(
            jax.ShapeDtypeStruct((2, R, R), jnp.float32),
            jax.ShapeDtypeStruct((1, R, R), jnp.float32),
        ),
        name="transfer",
    )(own_gram, every_group, upper)
    return (leaf_basis, transfer_leaf, transfer_group)


def solution(mesh):
    in_specs = (
        P(("grp", "dev"), None, None),
        P(("grp", "dev"), None, None),
        P(("grp", "dev"), None, None),
        P(("grp", "dev"), None),
        P(("grp", "dev")),
        P(("grp", "dev")),
    )
    out_specs = (P(("grp", "dev"), None, None), P(("grp", "dev"), None, None), P("grp", None, None))
    return jax.shard_map(body, mesh=mesh, in_specs=in_specs, out_specs=out_specs, check_vma=False)
```

```python
import functools
import math

import jax
import jax.numpy as jnp
from jax import lax
from jax.experimental import pallas as pl
from jax.experimental.pallas import tpu as pltpu
from jax.sharding import PartitionSpec as P

NZ, NX = 8, 4
R = 32
LEAF = 1024
PARTS = (("x", 0, 640, 0), ("z", 640, 384, 0), ("x", 0, 640, 1), ("z", 640, 384, 1))
GROUP = 4
HIGHEST = lax.Precision.HIGHEST
X_ORDER, Z_ORDER = (0, 2, 3, 1), (0, 4, 6, 1, 3, 7, 5, 2)


def halves(value):
    high = value.astype(jnp.bfloat16)
    low = (value - high.astype(jnp.float32)).astype(jnp.bfloat16)
    return high, low


def lookup(table, index):
    packed = sum(entry << (4 * i) for i, entry in enumerate(table))
    return (jnp.int32(packed) >> (4 * index)) & 15


def x_partner(step, core, x):
    q = (x - core) % NX
    return ((q ^ 1 if step == 0 else q ^ 3) + core) % NX


def z_partner(step, core, z):
    w = (z - core) % NZ
    odd = w % 2
    other = (w ^ 1, w - 1 + 2 * odd, w + 3 + 2 * odd)[step]
    return (other + core) % NZ


def contribution_kernel(rows_hbm, count_hbm, u_hbm, v_hbm, sketch_hbm, *refs):
    outs, scratch = refs[: 2 * len(PARTS)], refs[2 * len(PARTS) :]
    rows_ref, count_ref, u_ref, v_ref, sketch_ref, value_ref, sems = scratch
    slots = u_ref.shape[0]
    groups = slots // GROUP
    small = [
        pltpu.make_async_copy(rows_hbm, rows_ref, sems.at[0]),
        pltpu.make_async_copy(count_hbm, count_ref, sems.at[1]),
        pltpu.make_async_copy(sketch_hbm, sketch_ref, sems.at[2]),
    ]
    large = [
        [
            pltpu.make_async_copy(
                hbm.at[pl.ds(g * GROUP, GROUP)],
                ref.at[pl.ds(g * GROUP, GROUP)],
                sems.at[3 + 2 * g + k],
            )
            for k, (hbm, ref) in enumerate(((v_hbm, v_ref), (u_hbm, u_ref)))
        ]
        for g in range(groups)
    ]
    for copy in small + sum(large, []):
        copy.start()
    for ref in outs:
        ref[...] = jnp.zeros_like(ref)
    core = lax.axis_index("grp") % 2
    me = lax.axis_index("dev")
    own_w = (me // NX - core) & (NZ - 1)
    own_q = (me % NX - core) & (NX - 1)
    for copy in small:
        copy.wait()
    first_count = count_ref[0]
    live_count = first_count + count_ref[1]
    sketch_high, sketch_low = halves(sketch_ref[...].reshape(2 * R, LEAF))
    both = jnp.concatenate([sketch_high, sketch_low], axis=0)
    contract = (((1,), (1,)), ((), ()))
    for g in range(groups):
        large[g][0].wait()
        v_high, v_low = halves(v_ref[g * GROUP : (g + 1) * GROUP].reshape(GROUP * R, LEAF))
        wide = lax.dot_general(v_high, both, contract, preferred_element_type=jnp.float32)
        couplings = (
            wide[:, : 2 * R]
            + wide[:, 2 * R :]
            + lax.dot_general(v_low, sketch_high, contract, preferred_element_type=jnp.float32)
        )
        large[g][1].wait()
        for t in range(GROUP):
            part = couplings[t * R : (t + 1) * R]
            coupling = jnp.where(g * GROUP + t < first_count, part[:, :R], part[:, R:])
            c_high, c_low = halves(coupling)
            u_high, u_low = halves(u_ref[g * GROUP + t])
            left = jnp.concatenate([c_high, c_low, c_high], axis=0)
            right = jnp.concatenate([u_high, u_high, u_low], axis=0)
            value_ref[t] = lax.dot_general(
                left, right, (((0,), (0,)), ((), ())), preferred_element_type=jnp.float32
            )
        for t in range(GROUP):
            slot = g * GROUP + t
            row = rows_ref[slot] & (2 * NZ * NX - 1)
            cluster = row & 1
            live = slot < live_count
            to_q = (((row >> 1) & (NX - 1)) - core) & (NX - 1)
            to_w = ((row >> 3) - core) & (NZ - 1)
            step_z = jnp.where(own_w & 1 == 0, to_w - own_w, own_w - to_w) & (NZ - 1)
            x_slot, z_slot = lookup(X_ORDER, own_q ^ to_q), lookup(Z_ORDER, step_z)
            index = {"x": x_slot * NZ + z_slot, "z": z_slot * NX + x_slot}
            for k, (axis, start, width, which) in enumerate(PARTS):
                for far in range(2):
                    here = live & (index[axis] >> 4 == far)
                    if which >= 0:
                        here = here & (cluster == which)

                    @pl.when(here)
                    def _():
                        at = index[axis] & 15
                        first = pl.multiple_of(cluster * R, R) if which < 0 else 0
                        outs[2 * k + far][at, pl.ds(first, R)] += value_ref[
                            t, :, start : start + width
                        ]


def contributions(block_row, col_count, u_blocks, v_blocks, sketch):
    slots = u_blocks.shape[0]
    shapes = [
        jax.ShapeDtypeStruct((NZ * NX // 2, R if which >= 0 else 2 * R, width), jnp.float32)
        for _, _, width, which in PARTS
        for _ in range(2)
    ]
    return pl.pallas_call(
        contribution_kernel,
        out_shape=shapes,
        in_specs=[pl.BlockSpec(memory_space=pltpu.HBM)] * 5,
        out_specs=[pl.BlockSpec(memory_space=pltpu.VMEM)] * len(shapes),
        scratch_shapes=[
            pltpu.SMEM((slots,), jnp.int32),
            pltpu.SMEM((2,), jnp.int32),
            pltpu.VMEM((slots, R, LEAF), jnp.float32),
            pltpu.VMEM((slots, R, LEAF), jnp.float32),
            pltpu.VMEM((2, R, LEAF), jnp.float32),
            pltpu.VMEM((GROUP, R, LEAF), jnp.float32),
            pltpu.SemaphoreType.DMA((3 + 2 * (slots // GROUP),)),
        ],
        compiler_params=pltpu.CompilerParams(vmem_limit_bytes=24 << 20),
        cost_estimate=pl.CostEstimate(flops=10**9, bytes_accessed=16 << 20, transcendentals=0),
        name="contributions",
    )(block_row, col_count, u_blocks, v_blocks, sketch)


def exchange(value, axis, step):
    pairs = []
    groups = lax.axis_size("grp")
    for g in range(groups):
        for z in range(NZ):
            for x in range(NX):
                if axis == "x":
                    to = z * NX + x_partner(step, g % 2, x)
                else:
                    to = z_partner(step, g % 2, z) * NX + x
                pairs.append((g * NZ * NX + z * NX + x, g * NZ * NX + to))
    return lax.ppermute(value, ("grp", "dev"), pairs)


def scatter_sums(parts):
    order = {
        "x": (("x", 0), ("x", 1), ("z", 0), ("z", 1), ("z", 2)),
        "z": (("z", 0), ("z", 1), ("z", 2), ("x", 0), ("x", 1)),
    }
    terms = []
    for (first, _, _, _), (keep, send) in zip(PARTS, parts):
        for n, (axis, step) in enumerate(order[first]):
            got = exchange(send, axis, step)
            if n < 4:
                half = keep.shape[0] // 2
                send = keep[half:] + got[half:]
                keep = keep[:half] + got[:half]
        terms.append((keep[0], got[0]))
    return terms


def pack(gram):
    return jnp.concatenate([gram[8 * i : 8 * i + 8] for i in range(4)], axis=1)


def unpack(packed):
    return jnp.concatenate([packed[:, R * i : R * i + R] for i in range(4)], axis=0)


def eliminate(grams):
    count = len(grams)
    eye = (
        lax.broadcasted_iota(jnp.int32, (R, R), 0) == lax.broadcasted_iota(jnp.int32, (R, R), 1)
    ).astype(jnp.float32)
    work = [jnp.concatenate([gram, eye], axis=1) for gram in grams]
    sublane = lax.broadcasted_iota(jnp.int32, (R, 2 * R), 0)
    done = [jnp.zeros((R, 2 * R), jnp.float32) for _ in grams]
    for j in range(R):
        for i in range(count):
            column = jnp.broadcast_to(work[i][:, j : j + 1], (R, 2 * R))
            pivot = column[j : j + 1]
            scale = lax.rsqrt(pivot)
            scale = scale * (1.5 - 0.5 * pivot * scale * scale)
            row = jnp.broadcast_to(work[i][j : j + 1] * scale, (R, 2 * R))
            done[i] = jnp.where(sublane == j, row, done[i])
            work[i] = work[i] - (column * jnp.broadcast_to(scale, (R, 2 * R))) * row
    return [(d[:, :R], d[:, R:]) for d in done]


def sample_kernel(*refs):
    terms, (diag_ref, sketch_ref, sample_ref, gram_ref, packed_ref) = refs[:-5], refs[-5:]
    for k, (_, start, width, which) in enumerate(PARTS):
        far = terms[2 * k][...] + terms[2 * k + 1][...]
        for i in (0, 1) if which < 0 else (which,):
            rows = far[i * R : (i + 1) * R] if which < 0 else far
            columns = slice(start, start + width)
            sample_ref[i, :, columns] = (
                rows + diag_ref[i : i + 1, columns] * sketch_ref[i, :, columns]
            )
    total = jnp.zeros((R, R), jnp.float32)
    for i in range(2):
        sample = sample_ref[i]
        gram = lax.dot_general(
            sample,
            sample,
            (((1,), (1,)), ((), ())),
            precision=HIGHEST,
            preferred_element_type=jnp.float32,
        )
        gram_ref[i] = gram
        total = total + gram
    packed_ref[...] = jnp.broadcast_to(pack(total)[None], packed_ref.shape)


def leaf_kernel(gram_ref, sample_ref, basis_ref, upper_ref):
    factors = eliminate([gram_ref[0], gram_ref[1]])
    for i, (upper, inverse) in enumerate(factors):
        rows = lax.broadcasted_iota(jnp.int32, (R, R), 0)
        cols = lax.broadcasted_iota(jnp.int32, (R, R), 1)
        upper_ref[i] = jnp.where(rows <= cols, upper, 0.0)
        basis_ref[i] = jnp.dot(
            inverse * math.sqrt(LEAF),
            sample_ref[i],
            precision=HIGHEST,
            preferred_element_type=jnp.float32,
        )


def group_kernel(every_ref, packed_ref):
    packed_ref[...] = jnp.broadcast_to(jnp.sum(every_ref[...], axis=0)[None], packed_ref.shape)


def transfer_kernel(leaves, own_ref, every_ref, upper_ref, leaf_ref, group_ref):
    groups = every_ref.shape[0]
    group_gram = unpack(own_ref[0])
    root_gram = unpack(jnp.sum(every_ref[...], axis=0))
    (group_upper, group_inverse), (_, root_inverse) = eliminate([group_gram, root_gram])
    rows = lax.broadcasted_iota(jnp.int32, (R, R), 0)
    cols = lax.broadcasted_iota(jnp.int32, (R, R), 1)
    group_upper = jnp.where(rows <= cols, group_upper, 0.0)
    contract = (((1,), (1,)), ((), ()))
    for i in range(2):
        leaf_ref[i] = lax.dot_general(
            upper_ref[i],
            group_inverse * math.sqrt(leaves),
            contract,
            precision=HIGHEST,
            preferred_element_type=jnp.float32,
        )
    group_ref[0] = lax.dot_general(
        group_upper,
        root_inverse * math.sqrt(groups),
        contract,
        precision=HIGHEST,
        preferred_element_type=jnp.float32,
    )


def body(u_blocks, v_blocks, sketch, near_diag, block_row, col_count):
    members = lax.axis_size("dev")
    groups = lax.axis_size("grp")
    halved = contributions(block_row, col_count, u_blocks, v_blocks, sketch)
    terms = scatter_sums(list(zip(halved[::2], halved[1::2])))
    sample, gram, packed = pl.pallas_call(
        sample_kernel,
        out_shape=(
            jax.ShapeDtypeStruct((2, R, LEAF), jnp.float32),
            jax.ShapeDtypeStruct((2, R, R), jnp.float32),
            jax.ShapeDtypeStruct((members, 8, 128), jnp.float32),
        ),
        name="sample",
    )(*sum(terms, ()), near_diag, sketch)
    every = lax.all_to_all(packed, "dev", split_axis=0, concat_axis=0, tiled=True)
    leaf_basis, upper = pl.pallas_call(
        leaf_kernel,
        out_shape=(
            jax.ShapeDtypeStruct((2, R, LEAF), jnp.float32),
            jax.ShapeDtypeStruct((2, R, R), jnp.float32),
        ),
        name="leaf",
    )(gram, sample)
    own_gram = pl.pallas_call(
        group_kernel,
        out_shape=jax.ShapeDtypeStruct((groups, 8, 128), jnp.float32),
        name="group",
    )(every)
    every_group = lax.all_to_all(own_gram, "grp", split_axis=0, concat_axis=0, tiled=True)
    transfer_leaf, transfer_group = pl.pallas_call(
        functools.partial(transfer_kernel, 2 * members),
        out_shape=(
            jax.ShapeDtypeStruct((2, R, R), jnp.float32),
            jax.ShapeDtypeStruct((1, R, R), jnp.float32),
        ),
        name="transfer",
    )(own_gram, every_group, upper)
    return (leaf_basis, transfer_leaf, transfer_group)


def solution(mesh):
    in_specs = (
        P(("grp", "dev"), None, None),
        P(("grp", "dev"), None, None),
        P(("grp", "dev"), None, None),
        P(("grp", "dev"), None),
        P(("grp", "dev")),
        P(("grp", "dev")),
    )
    out_specs = (P(("grp", "dev"), None, None), P(("grp", "dev"), None, None), P("grp", None, None))
    return jax.shard_map(body, mesh=mesh, in_specs=in_specs, out_specs=out_specs, check_vma=False)
```

```python
import functools
import math

import jax
import jax.numpy as jnp
from jax import lax
from jax.experimental import pallas as pl
from jax.experimental.pallas import tpu as pltpu
from jax.sharding import PartitionSpec as P

NZ, NX = 8, 4
R = 32
LEAF = 1024
PARTS = (("x", 0, 512, 0), ("z", 512, 512, 0), ("x", 0, 512, 1), ("z", 512, 512, 1))
STEPS = {
    "x": (("x", 0), ("x", 1), ("z", 0), ("z", 1)),
    "z": (("z", 0), ("z", 1), ("x", 0), ("x", 1)),
}
BLOCK = 4
GROUP = 4
HIGHEST = lax.Precision.HIGHEST
X_ORDER, Z_ORDER = (0, 2, 3, 1), (0, 4, 6, 1, 3, 7, 5, 2)


def halves(value):
    high = value.astype(jnp.bfloat16)
    low = (value - high.astype(jnp.float32)).astype(jnp.bfloat16)
    return high, low


def lookup(table, index):
    packed = sum(entry << (4 * i) for i, entry in enumerate(table))
    return (jnp.int32(packed) >> (4 * index)) & 15


def x_partner(step, which, x):
    q = (x - which) % NX
    return ((q ^ 1 if step == 0 else q ^ 3) + which) % NX


def z_partner(step, which, z):
    w = (z - which) % NZ
    odd = w % 2
    other = (w ^ 1, w - 1 + 2 * odd, w + 3 + 2 * odd)[step]
    return (other + which) % NZ


def contribution_kernel(rows_hbm, count_hbm, u_hbm, v_hbm, sketch_hbm, *refs):
    outs, scratch = refs[: 2 * len(PARTS)], refs[2 * len(PARTS) :]
    rows_ref, count_ref, u_ref, v_ref, sketch_ref, value_ref, sems = scratch
    slots = u_ref.shape[0]
    groups = slots // GROUP
    small = [
        pltpu.make_async_copy(rows_hbm, rows_ref, sems.at[0]),
        pltpu.make_async_copy(count_hbm, count_ref, sems.at[1]),
        pltpu.make_async_copy(sketch_hbm, sketch_ref, sems.at[2]),
    ]
    large = [
        [
            pltpu.make_async_copy(
                hbm.at[pl.ds(g * GROUP, GROUP)],
                ref.at[pl.ds(g * GROUP, GROUP)],
                sems.at[3 + 2 * g + k],
            )
            for k, (hbm, ref) in enumerate(((v_hbm, v_ref), (u_hbm, u_ref)))
        ]
        for g in range(groups)
    ]
    for copy in small + sum(large, []):
        copy.start()
    for ref in outs:
        ref[...] = jnp.zeros_like(ref)
    me = lax.axis_index("dev")
    for copy in small:
        copy.wait()
    first_count = count_ref[0]
    live_count = first_count + count_ref[1]
    sketch_high, sketch_low = halves(sketch_ref[...].reshape(2 * R, LEAF))
    both = jnp.concatenate([sketch_high, sketch_low], axis=0)
    contract = (((1,), (1,)), ((), ()))
    for g in range(groups):
        large[g][0].wait()
        v_high, v_low = halves(v_ref[g * GROUP : (g + 1) * GROUP].reshape(GROUP * R, LEAF))
        wide = lax.dot_general(v_high, both, contract, preferred_element_type=jnp.float32)
        couplings = (
            wide[:, : 2 * R]
            + wide[:, 2 * R :]
            + lax.dot_general(v_low, sketch_high, contract, preferred_element_type=jnp.float32)
        )
        large[g][1].wait()
        for t in range(GROUP):
            part = couplings[t * R : (t + 1) * R]
            coupling = jnp.where(g * GROUP + t < first_count, part[:, :R], part[:, R:])
            c_high, c_low = halves(coupling)
            u_high, u_low = halves(u_ref[g * GROUP + t])
            left = jnp.concatenate([c_high, c_low, c_high], axis=0)
            right = jnp.concatenate([u_high, u_high, u_low], axis=0)
            value_ref[t] = lax.dot_general(
                left, right, (((0,), (0,)), ((), ())), preferred_element_type=jnp.float32
            )
        for t in range(GROUP):
            slot = g * GROUP + t
            row = rows_ref[slot] & (2 * NZ * NX - 1)
            cluster = row & 1
            live = slot < live_count
            own_w = (me // NX - cluster) & (NZ - 1)
            own_q = (me % NX - cluster) & (NX - 1)
            to_w = ((row >> 3) - cluster) & (NZ - 1)
            to_q = (((row >> 1) & (NX - 1)) - cluster) & (NX - 1)
            step_z = jnp.where(own_w & 1 == 0, to_w - own_w, own_w - to_w) & (NZ - 1)
            x_slot, z_slot = lookup(X_ORDER, own_q ^ to_q), lookup(Z_ORDER, step_z)
            index = {
                "x": x_slot * NZ + z_slot,
                "z": (z_slot >> 1) * 2 * NX + x_slot * 2 + (z_slot & 1),
            }
            for k, (axis, start, width, which) in enumerate(PARTS):
                for far in range(2):

                    @pl.when(live & (index[axis] >> 4 == far) & (cluster == which))
                    def _():
                        outs[2 * k + far][index[axis] & 15] += value_ref[
                            t, :, start : start + width
                        ]


def in_hbm(value):
    return pltpu.with_memory_space_constraint(value, pltpu.HBM)


def in_vmem(count):
    return [pl.BlockSpec(memory_space=pltpu.VMEM)] * count


def contributions(block_row, col_count, u_blocks, v_blocks, sketch):
    slots = u_blocks.shape[0]
    shapes = [
        jax.ShapeDtypeStruct((NZ * NX // 2, R, width), jnp.float32)
        for _, _, width, _ in PARTS
        for _ in range(2)
    ]
    return pl.pallas_call(
        contribution_kernel,
        out_shape=shapes,
        in_specs=[pl.BlockSpec(memory_space=pltpu.HBM)] * 5,
        out_specs=in_vmem(len(shapes)),
        scratch_shapes=[
            pltpu.SMEM((slots,), jnp.int32),
            pltpu.SMEM((2,), jnp.int32),
            pltpu.VMEM((slots, R, LEAF), jnp.float32),
            pltpu.VMEM((slots, R, LEAF), jnp.float32),
            pltpu.VMEM((2, R, LEAF), jnp.float32),
            pltpu.VMEM((GROUP, R, LEAF), jnp.float32),
            pltpu.SemaphoreType.DMA((3 + 2 * (slots // GROUP),)),
        ],
        compiler_params=pltpu.CompilerParams(vmem_limit_bytes=24 << 20),
        cost_estimate=pl.CostEstimate(flops=10**9, bytes_accessed=16 << 20, transcendentals=0),
        name="contributions",
    )(*(in_hbm(a) for a in (block_row, col_count, u_blocks, v_blocks, sketch)))


def exchange(value, axis, step, which):
    pairs = []
    for z in range(NZ):
        for x in range(NX):
            if axis == "x":
                to = z * NX + x_partner(step, which, x)
            else:
                to = z_partner(step, which, z) * NX + x
            pairs.append((z * NX + x, to))
    return lax.ppermute(value, "dev", pairs)


def scatter_sums(parts):
    kept, last = [], []
    for (first, _, _, which), (keep, send) in zip(PARTS, parts):
        for axis, step in STEPS[first]:
            got = exchange(send, axis, step, which)
            half = keep.shape[0] // 2
            send = keep[half:] + got[half:]
            keep = keep[:half] + got[:half]
        kept.append(keep[0])
        last.append(send)
    terms = []
    for i in range(0, len(PARTS), 2):
        got = exchange(jnp.concatenate(last[i : i + 2], axis=2), "z", 2, PARTS[i][3])
        terms += kept[i : i + 2] + [got[0]]
    return terms


def pack(gram):
    return jnp.concatenate([gram[8 * i : 8 * i + 8] for i in range(4)], axis=1)


def unpack(packed):
    return jnp.concatenate([packed[:, R * i : R * i + R] for i in range(4)], axis=0)


def eliminate(grams):
    eye = (
        lax.broadcasted_iota(jnp.int32, (R, R), 0) == lax.broadcasted_iota(jnp.int32, (R, R), 1)
    ).astype(jnp.float32)
    wide = (R, 2 * R)
    work = [jnp.concatenate([gram, eye], axis=1) for gram in grams]
    done = [[] for _ in grams]
    for first in range(0, R, BLOCK):
        columns = [
            [jnp.broadcast_to(w[:, j : j + 1], wide) for j in range(first, first + BLOCK)]
            for w in work
        ]
        for j in range(first, first + BLOCK):
            for i in range(len(grams)):
                column = columns[i][j - first]
                pivot = column[j : j + 1]
                scale = lax.rsqrt(pivot)
                scale = scale * (1.5 - 0.5 * pivot * scale * scale)
                row = work[i][j : j + 1] * scale
                done[i].append(row)
                factor = column * jnp.broadcast_to(scale, wide)
                for k in range(j + 1, first + BLOCK):
                    entry = columns[i][k - first]
                    columns[i][k - first] = entry - factor * jnp.broadcast_to(
                        entry[j : j + 1] * scale, wide
                    )
                work[i] = work[i] - factor * jnp.broadcast_to(row, wide)
    whole = [jnp.concatenate(rows, axis=0) for rows in done]
    return [(d[:, :R], d[:, R:]) for d in whole]


def sample_kernel(*refs):
    terms, (diag_ref, sketch_ref, sample_ref, gram_ref, packed_ref) = refs[:-5], refs[-5:]
    for k, (_, start, width, which) in enumerate(PARTS):
        columns = slice(start, start + width)
        far = terms[k // 2 * 3 + k % 2][...] + terms[k // 2 * 3 + 2][:, columns]
        near = diag_ref[which : which + 1, columns] * sketch_ref[which, :, columns]
        sample_ref[which, :, columns] = far + near
    total = jnp.zeros((R, R), jnp.float32)
    for i in range(2):
        sample = sample_ref[i]
        gram = lax.dot_general(
            sample,
            sample,
            (((1,), (1,)), ((), ())),
            precision=HIGHEST,
            preferred_element_type=jnp.float32,
        )
        gram_ref[i] = gram
        total = total + gram
    packed_ref[...] = jnp.broadcast_to(pack(total)[None], packed_ref.shape)


def leaf_kernel(gram_ref, sample_ref, basis_ref, upper_ref):
    factors = eliminate([gram_ref[0], gram_ref[1]])
    for i, (upper, inverse) in enumerate(factors):
        rows = lax.broadcasted_iota(jnp.int32, (R, R), 0)
        cols = lax.broadcasted_iota(jnp.int32, (R, R), 1)
        upper_ref[i] = jnp.where(rows <= cols, upper, 0.0)
        basis_ref[i] = jnp.dot(
            inverse * math.sqrt(LEAF),
            sample_ref[i],
            precision=HIGHEST,
            preferred_element_type=jnp.float32,
        )


def group_kernel(every_ref, packed_ref):
    packed_ref[...] = jnp.broadcast_to(jnp.sum(every_ref[...], axis=0)[None], packed_ref.shape)


def transfer_kernel(leaves, own_ref, every_ref, upper_ref, leaf_ref, group_ref):
    groups = every_ref.shape[0]
    group_gram = unpack(own_ref[0])
    root_gram = unpack(jnp.sum(every_ref[...], axis=0))
    (group_upper, group_inverse), (_, root_inverse) = eliminate([group_gram, root_gram])
    rows = lax.broadcasted_iota(jnp.int32, (R, R), 0)
    cols = lax.broadcasted_iota(jnp.int32, (R, R), 1)
    group_upper = jnp.where(rows <= cols, group_upper, 0.0)
    contract = (((1,), (1,)), ((), ()))
    for i in range(2):
        leaf_ref[i] = lax.dot_general(
            upper_ref[i],
            group_inverse * math.sqrt(leaves),
            contract,
            precision=HIGHEST,
            preferred_element_type=jnp.float32,
        )
    group_ref[0] = lax.dot_general(
        group_upper,
        root_inverse * math.sqrt(groups),
        contract,
        precision=HIGHEST,
        preferred_element_type=jnp.float32,
    )


def body(u_blocks, v_blocks, sketch, near_diag, block_row, col_count):
    members = lax.axis_size("dev")
    groups = lax.axis_size("grp")
    halved = contributions(block_row, col_count, u_blocks, v_blocks, sketch)
    terms = scatter_sums(list(zip(halved[::2], halved[1::2])))
    sample, gram, packed = pl.pallas_call(
        sample_kernel,
        out_shape=(
            jax.ShapeDtypeStruct((2, R, LEAF), jnp.float32),
            jax.ShapeDtypeStruct((2, R, R), jnp.float32),
            jax.ShapeDtypeStruct((members, 8, 128), jnp.float32),
        ),
        in_specs=in_vmem(len(terms) + 2),
        out_specs=in_vmem(3),
        name="sample",
    )(*terms, near_diag, sketch)
    every = lax.all_to_all(packed, "dev", split_axis=0, concat_axis=0, tiled=True)
    leaf_basis, upper = pl.pallas_call(
        leaf_kernel,
        out_shape=(
            jax.ShapeDtypeStruct((2, R, LEAF), jnp.float32),
            jax.ShapeDtypeStruct((2, R, R), jnp.float32),
        ),
        in_specs=in_vmem(2),
        out_specs=[pl.BlockSpec((2, R, LEAF), lambda: (0, 0, 0))] + in_vmem(1),
        name="leaf",
    )(gram, sample)
    own_gram = pl.pallas_call(
        group_kernel,
        out_shape=jax.ShapeDtypeStruct((groups, 8, 128), jnp.float32),
        in_specs=in_vmem(1),
        out_specs=pl.BlockSpec(memory_space=pltpu.VMEM),
        name="group",
    )(every)
    every_group = lax.all_to_all(own_gram, "grp", split_axis=0, concat_axis=0, tiled=True)
    transfer_leaf, transfer_group = pl.pallas_call(
        functools.partial(transfer_kernel, 2 * members),
        out_shape=(
            jax.ShapeDtypeStruct((2, R, R), jnp.float32),
            jax.ShapeDtypeStruct((1, R, R), jnp.float32),
        ),
        in_specs=in_vmem(3),
        name="transfer",
    )(own_gram, every_group, upper)
    return (leaf_basis, transfer_leaf, transfer_group)


def solution(mesh):
    in_specs = (
        P(("grp", "dev"), None, None),
        P(("grp", "dev"), None, None),
        P(("grp", "dev"), None, None),
        P(("grp", "dev"), None),
        P(("grp", "dev")),
        P(("grp", "dev")),
    )
    out_specs = (P(("grp", "dev"), None, None), P(("grp", "dev"), None, None), P("grp", None, None))
    return jax.shard_map(body, mesh=mesh, in_specs=in_specs, out_specs=out_specs, check_vma=False)
```

```python
import functools
import math

import jax
import jax.numpy as jnp
from jax import lax
from jax.experimental import pallas as pl
from jax.experimental.pallas import tpu as pltpu
from jax.sharding import PartitionSpec as P

NZ, NX = 8, 4
NY = 4
R = 32
LEAF = 1024
PARTS = (("x", 0, 512, 0), ("z", 512, 512, 0), ("x", 0, 512, 1), ("z", 512, 512, 1))
STEPS = {
    "x": (("x", 0), ("x", 1), ("z", 0), ("z", 1)),
    "z": (("z", 0), ("z", 1), ("x", 0), ("x", 1)),
}
BLOCK = 4
GROUP = 4
HIGHEST = lax.Precision.HIGHEST
X_ORDER, Z_ORDER = (0, 2, 3, 1), (0, 4, 6, 1, 3, 7, 5, 2)


def halves(value):
    high = value.astype(jnp.bfloat16)
    low = (value - high.astype(jnp.float32)).astype(jnp.bfloat16)
    return high, low


def lookup(table, index):
    packed = sum(entry << (4 * i) for i, entry in enumerate(table))
    return (jnp.int32(packed) >> (4 * index)) & 15


def x_partner(step, which, x):
    q = (x - which) % NX
    return ((q ^ 1 if step == 0 else q ^ 3) + which) % NX


def z_partner(step, which, z):
    w = (z - which) % NZ
    odd = w % 2
    other = (w ^ 1, w - 1 + 2 * odd, w + 3 + 2 * odd)[step]
    return (other + which) % NZ


def contribution_kernel(rows_hbm, count_hbm, u_hbm, v_hbm, sketch_hbm, *refs):
    outs, scratch = refs[: 2 * len(PARTS)], refs[2 * len(PARTS) :]
    rows_ref, count_ref, u_ref, v_ref, sketch_ref, value_ref, sems = scratch
    slots = u_ref.shape[0]
    groups = slots // GROUP
    small = [
        pltpu.make_async_copy(rows_hbm, rows_ref, sems.at[0]),
        pltpu.make_async_copy(count_hbm, count_ref, sems.at[1]),
        pltpu.make_async_copy(sketch_hbm, sketch_ref, sems.at[2]),
    ]
    large = [pltpu.make_async_copy(v_hbm, v_ref, sems.at[3])] + [
        pltpu.make_async_copy(
            u_hbm.at[pl.ds(g * GROUP, GROUP)], u_ref.at[pl.ds(g * GROUP, GROUP)], sems.at[4 + g]
        )
        for g in range(groups)
    ]
    for copy in small + large:
        copy.start()
    for ref in outs:
        ref[...] = jnp.zeros_like(ref)
    me = lax.axis_index("dev")
    for copy in small:
        copy.wait()
    first_count = count_ref[0]
    live_count = first_count + count_ref[1]
    sketch_high, sketch_low = halves(sketch_ref[...].reshape(2 * R, LEAF))
    both = jnp.concatenate([sketch_high, sketch_low], axis=0)
    contract = (((1,), (1,)), ((), ()))
    large[0].wait()
    v_high, v_low = halves(v_ref[...].reshape(slots * R, LEAF))
    wide = lax.dot_general(v_high, both, contract, preferred_element_type=jnp.float32)
    couplings = (
        wide[:, : 2 * R]
        + wide[:, 2 * R :]
        + lax.dot_general(v_low, sketch_high, contract, preferred_element_type=jnp.float32)
    )
    for g in range(groups):
        large[1 + g].wait()
        for t in range(GROUP):
            part = couplings[(g * GROUP + t) * R : (g * GROUP + t + 1) * R]
            coupling = jnp.where(g * GROUP + t < first_count, part[:, :R], part[:, R:])
            c_high, c_low = halves(coupling)
            u_high, u_low = halves(u_ref[g * GROUP + t])
            left = jnp.concatenate([c_high, c_low, c_high], axis=0)
            right = jnp.concatenate([u_high, u_high, u_low], axis=0)
            value_ref[t] = lax.dot_general(
                left, right, (((0,), (0,)), ((), ())), preferred_element_type=jnp.float32
            )
        for t in range(GROUP):
            slot = g * GROUP + t
            row = rows_ref[slot] & (2 * NZ * NX - 1)
            cluster = row & 1
            live = slot < live_count
            own_w = (me // NX - cluster) & (NZ - 1)
            own_q = (me % NX - cluster) & (NX - 1)
            to_w = ((row >> 3) - cluster) & (NZ - 1)
            to_q = (((row >> 1) & (NX - 1)) - cluster) & (NX - 1)
            step_z = jnp.where(own_w & 1 == 0, to_w - own_w, own_w - to_w) & (NZ - 1)
            x_slot, z_slot = lookup(X_ORDER, own_q ^ to_q), lookup(Z_ORDER, step_z)
            index = {
                "x": x_slot * NZ + z_slot,
                "z": (z_slot >> 1) * 2 * NX + x_slot * 2 + (z_slot & 1),
            }
            for k, (axis, start, width, which) in enumerate(PARTS):
                for far in range(2):

                    @pl.when(live & (index[axis] >> 4 == far) & (cluster == which))
                    def _():
                        outs[2 * k + far][index[axis] & 15] += value_ref[
                            t, :, start : start + width
                        ]


def in_hbm(value):
    return pltpu.with_memory_space_constraint(value, pltpu.HBM)


def in_vmem(count):
    return [pl.BlockSpec(memory_space=pltpu.VMEM)] * count


def pin(*values):
    return [pltpu.with_memory_space_constraint(value, pltpu.VMEM) for value in values]


def contributions(block_row, col_count, u_blocks, v_blocks, sketch):
    slots = u_blocks.shape[0]
    shapes = [
        jax.ShapeDtypeStruct((NZ * NX // 2, R, width), jnp.float32)
        for _, _, width, _ in PARTS
        for _ in range(2)
    ]
    return pl.pallas_call(
        contribution_kernel,
        out_shape=shapes,
        in_specs=[pl.BlockSpec(memory_space=pltpu.HBM)] * 5,
        out_specs=in_vmem(len(shapes)),
        scratch_shapes=[
            pltpu.SMEM((slots,), jnp.int32),
            pltpu.SMEM((2,), jnp.int32),
            pltpu.VMEM((slots, R, LEAF), jnp.float32),
            pltpu.VMEM((slots, R, LEAF), jnp.float32),
            pltpu.VMEM((2, R, LEAF), jnp.float32),
            pltpu.VMEM((GROUP, R, LEAF), jnp.float32),
            pltpu.SemaphoreType.DMA((4 + slots // GROUP,)),
        ],
        compiler_params=pltpu.CompilerParams(vmem_limit_bytes=24 << 20),
        cost_estimate=pl.CostEstimate(flops=10**9, bytes_accessed=16 << 20, transcendentals=0),
        name="contributions",
    )(*(in_hbm(a) for a in (block_row, col_count, u_blocks, v_blocks, sketch)))


def exchange(value, axis, step, which):
    pairs = []
    for z in range(NZ):
        for x in range(NX):
            if axis == "x":
                to = z * NX + x_partner(step, which, x)
            else:
                to = z_partner(step, which, z) * NX + x
            pairs.append((z * NX + x, to))
    return lax.ppermute(value, "dev", pairs)


def across(value, step):
    pairs = []
    for g in range(2 * NY):
        y, core = g // 2, g % 2
        to = (g ^ 1, 2 * (y ^ 1) + core, 2 * (y ^ 3) + core)[step]
        pairs.append((g, to))
    return lax.ppermute(value, "grp", pairs)


def scatter_sums(parts):
    kept, last = [], []
    for (first, _, _, which), (keep, send) in zip(PARTS, parts):
        for axis, step in STEPS[first]:
            got = exchange(send, axis, step, which)
            half = keep.shape[0] // 2
            send = keep[half:] + got[half:]
            keep = keep[:half] + got[:half]
        kept.append(keep[0])
        last.append(send)
    terms = []
    for i in range(0, len(PARTS), 2):
        got = exchange(jnp.concatenate(last[i : i + 2], axis=2), "z", 2, PARTS[i][3])
        terms += kept[i : i + 2] + [got[0]]
    return terms


def pack(gram):
    return jnp.concatenate([gram[8 * i : 8 * i + 8] for i in range(4)], axis=1)


def unpack(packed):
    return jnp.concatenate([packed[:, R * i : R * i + R] for i in range(4)], axis=0)


def eliminate(grams):
    eye = (
        lax.broadcasted_iota(jnp.int32, (R, R), 0) == lax.broadcasted_iota(jnp.int32, (R, R), 1)
    ).astype(jnp.float32)
    wide = (R, 2 * R)
    work = [jnp.concatenate([gram, eye], axis=1) for gram in grams]
    done = [[] for _ in grams]
    for first in range(0, R, BLOCK):
        columns = [
            [jnp.broadcast_to(w[:, j : j + 1], wide) for j in range(first, first + BLOCK)]
            for w in work
        ]
        for j in range(first, first + BLOCK):
            for i in range(len(grams)):
                column = columns[i][j - first]
                pivot = column[j : j + 1]
                scale = lax.rsqrt(pivot)
                scale = scale * (1.5 - 0.5 * pivot * scale * scale)
                row = work[i][j : j + 1] * scale
                done[i].append(row)
                factor = column * jnp.broadcast_to(scale, wide)
                for k in range(j + 1, first + BLOCK):
                    entry = columns[i][k - first]
                    columns[i][k - first] = entry - factor * jnp.broadcast_to(
                        entry[j : j + 1] * scale, wide
                    )
                work[i] = work[i] - factor * jnp.broadcast_to(row, wide)
    whole = [jnp.concatenate(rows, axis=0) for rows in done]
    return [(d[:, :R], d[:, R:]) for d in whole]


def sample_kernel(*refs):
    terms, (diag_ref, sketch_ref, sample_ref, gram_ref, packed_ref) = refs[:-5], refs[-5:]
    for k, (_, start, width, which) in enumerate(PARTS):
        columns = slice(start, start + width)
        far = terms[k // 2 * 3 + k % 2][...] + terms[k // 2 * 3 + 2][:, columns]
        near = diag_ref[which : which + 1, columns] * sketch_ref[which, :, columns]
        sample_ref[which, :, columns] = far + near
    total = jnp.zeros((R, R), jnp.float32)
    for i in range(2):
        sample = sample_ref[i]
        gram = lax.dot_general(
            sample,
            sample,
            (((1,), (1,)), ((), ())),
            precision=HIGHEST,
            preferred_element_type=jnp.float32,
        )
        gram_ref[i] = gram
        total = total + gram
    packed_ref[...] = jnp.broadcast_to(pack(total)[None], packed_ref.shape)


def leaf_kernel(gram_ref, sample_ref, basis_ref, upper_ref):
    factors = eliminate([gram_ref[0], gram_ref[1]])
    for i, (upper, inverse) in enumerate(factors):
        rows = lax.broadcasted_iota(jnp.int32, (R, R), 0)
        cols = lax.broadcasted_iota(jnp.int32, (R, R), 1)
        upper_ref[i] = jnp.where(rows <= cols, upper, 0.0)
        basis_ref[i] = jnp.dot(
            inverse * math.sqrt(LEAF),
            sample_ref[i],
            precision=HIGHEST,
            preferred_element_type=jnp.float32,
        )


def group_kernel(every_ref, packed_ref):
    packed_ref[...] = jnp.sum(every_ref[...], axis=0)


def transfer_kernel(leaves, groups, own_ref, near_ref, far_ref, upper_ref, leaf_ref, group_ref):
    group_gram = unpack(own_ref[...])
    root_gram = unpack(near_ref[...] + far_ref[...])
    (group_upper, group_inverse), (_, root_inverse) = eliminate([group_gram, root_gram])
    rows = lax.broadcasted_iota(jnp.int32, (R, R), 0)
    cols = lax.broadcasted_iota(jnp.int32, (R, R), 1)
    group_upper = jnp.where(rows <= cols, group_upper, 0.0)
    contract = (((1,), (1,)), ((), ()))
    for i in range(2):
        leaf_ref[i] = lax.dot_general(
            upper_ref[i],
            group_inverse * math.sqrt(leaves),
            contract,
            precision=HIGHEST,
            preferred_element_type=jnp.float32,
        )
    group_ref[0] = lax.dot_general(
        group_upper,
        root_inverse * math.sqrt(groups),
        contract,
        precision=HIGHEST,
        preferred_element_type=jnp.float32,
    )


def body(u_blocks, v_blocks, sketch, near_diag, block_row, col_count):
    members = lax.axis_size("dev")
    groups = lax.axis_size("grp")
    halved = contributions(block_row, col_count, u_blocks, v_blocks, sketch)
    terms = scatter_sums(list(zip(halved[::2], halved[1::2])))
    sample, gram, packed = pl.pallas_call(
        sample_kernel,
        out_shape=(
            pltpu.VMEM((2, R, LEAF), jnp.float32),
            pltpu.VMEM((2, R, R), jnp.float32),
            jax.ShapeDtypeStruct((members, 8, 128), jnp.float32),
        ),
        in_specs=in_vmem(len(terms) + 2),
        out_specs=in_vmem(3),
        name="sample",
    )(*pin(*terms), near_diag, sketch)
    every = lax.all_to_all(packed, "dev", split_axis=0, concat_axis=0, tiled=True)
    leaf_basis, upper = pl.pallas_call(
        leaf_kernel,
        out_shape=(
            jax.ShapeDtypeStruct((2, R, LEAF), jnp.float32),
            pltpu.VMEM((2, R, R), jnp.float32),
        ),
        in_specs=in_vmem(2),
        out_specs=[pl.BlockSpec((2, R, LEAF), lambda: (0, 0, 0))] + in_vmem(1),
        name="leaf",
    )(*pin(gram, sample))
    own_gram = pl.pallas_call(
        group_kernel,
        out_shape=pltpu.VMEM((8, 128), jnp.float32),
        in_specs=in_vmem(1),
        out_specs=pl.BlockSpec(memory_space=pltpu.VMEM),
        name="group",
    )(*pin(every))
    total, got = own_gram, across(own_gram, 0)
    for step in range(1, 3):
        total = total + got
        got = across(total, step)
    transfer_leaf, transfer_group = pl.pallas_call(
        functools.partial(transfer_kernel, 2 * members, groups),
        out_shape=(
            jax.ShapeDtypeStruct((2, R, R), jnp.float32),
            jax.ShapeDtypeStruct((1, R, R), jnp.float32),
        ),
        in_specs=in_vmem(4),
        name="transfer",
    )(*pin(own_gram, total, got, upper))
    return (leaf_basis, transfer_leaf, transfer_group)


def solution(mesh):
    in_specs = (
        P(("grp", "dev"), None, None),
        P(("grp", "dev"), None, None),
        P(("grp", "dev"), None, None),
        P(("grp", "dev"), None),
        P(("grp", "dev")),
        P(("grp", "dev")),
    )
    out_specs = (P(("grp", "dev"), None, None), P(("grp", "dev"), None, None), P("grp", None, None))
    return jax.shard_map(body, mesh=mesh, in_specs=in_specs, out_specs=out_specs, check_vma=False)
```

```python
import functools
import math

import jax
import jax.numpy as jnp
from jax import lax
from jax.experimental import pallas as pl
from jax.experimental.pallas import tpu as pltpu
from jax.sharding import PartitionSpec as P

NZ, NX = 8, 4
NY = 4
R = 32
LEAF = 1024
PARTS = (("x", 0, 512, 0), ("z", 512, 512, 0), ("x", 0, 512, 1), ("z", 512, 512, 1))
STEPS = {
    "x": (("x", 0), ("x", 1), ("z", 0), ("z", 1)),
    "z": (("z", 0), ("z", 1), ("x", 0), ("x", 1)),
}
BLOCK = 8
GROUP = 24
HIGHEST = lax.Precision.HIGHEST
X_ORDER, Z_ORDER = (0, 2, 3, 1), (0, 4, 6, 1, 3, 7, 5, 2)


def halves(value):
    high = value.astype(jnp.bfloat16)
    low = (value - high.astype(jnp.float32)).astype(jnp.bfloat16)
    return high, low


def lookup(table, index):
    packed = sum(entry << (4 * i) for i, entry in enumerate(table))
    return (jnp.int32(packed) >> (4 * index)) & 15


def x_partner(step, which, x):
    q = (x - which) % NX
    return ((q ^ 1 if step == 0 else q ^ 3) + which) % NX


def z_partner(step, which, z):
    w = (z - which) % NZ
    odd = w % 2
    other = (w ^ 1, w - 1 + 2 * odd, w + 3 + 2 * odd)[step]
    return (other + which) % NZ


def contribution_kernel(rows_hbm, count_hbm, u_hbm, v_hbm, sketch_hbm, *refs):
    outs, scratch = refs[: 2 * len(PARTS)], refs[2 * len(PARTS) :]
    rows_ref, count_ref, u_ref, v_ref, sketch_ref, value_ref, sems = scratch
    slots = u_ref.shape[0]
    groups = slots // GROUP
    small = [
        pltpu.make_async_copy(rows_hbm, rows_ref, sems.at[0]),
        pltpu.make_async_copy(count_hbm, count_ref, sems.at[1]),
        pltpu.make_async_copy(sketch_hbm, sketch_ref, sems.at[2]),
    ]
    large = [pltpu.make_async_copy(v_hbm, v_ref, sems.at[3])] + [
        pltpu.make_async_copy(
            u_hbm.at[pl.ds(g * GROUP, GROUP)], u_ref.at[pl.ds(g * GROUP, GROUP)], sems.at[4 + g]
        )
        for g in range(groups)
    ]
    for copy in small + large:
        copy.start()
    for ref in outs:
        ref[...] = jnp.zeros_like(ref)
    me = lax.axis_index("dev")
    for copy in small:
        copy.wait()
    first_count = count_ref[0]
    live_count = first_count + count_ref[1]
    sketch_high, sketch_low = halves(sketch_ref[...].reshape(2 * R, LEAF))
    both = jnp.concatenate([sketch_high, sketch_low], axis=0)
    contract = (((1,), (1,)), ((), ()))
    large[0].wait()
    v_high, v_low = halves(v_ref[...].reshape(slots * R, LEAF))
    wide = lax.dot_general(v_high, both, contract, preferred_element_type=jnp.float32)
    couplings = (
        wide[:, : 2 * R]
        + wide[:, 2 * R :]
        + lax.dot_general(v_low, sketch_high, contract, preferred_element_type=jnp.float32)
    )
    for g in range(groups):
        large[1 + g].wait()
        for t in range(GROUP):
            part = couplings[(g * GROUP + t) * R : (g * GROUP + t + 1) * R]
            coupling = jnp.where(g * GROUP + t < first_count, part[:, :R], part[:, R:])
            c_high, c_low = halves(coupling)
            u_high, u_low = halves(u_ref[g * GROUP + t])
            left = jnp.concatenate([c_high, c_low, c_high], axis=0)
            right = jnp.concatenate([u_high, u_high, u_low], axis=0)
            value_ref[t] = lax.dot_general(
                left, right, (((0,), (0,)), ((), ())), preferred_element_type=jnp.float32
            )
        for t in range(GROUP):
            slot = g * GROUP + t
            row = rows_ref[slot] & (2 * NZ * NX - 1)
            cluster = row & 1
            live = slot < live_count
            own_w = (me // NX - cluster) & (NZ - 1)
            own_q = (me % NX - cluster) & (NX - 1)
            to_w = ((row >> 3) - cluster) & (NZ - 1)
            to_q = (((row >> 1) & (NX - 1)) - cluster) & (NX - 1)
            step_z = jnp.where(own_w & 1 == 0, to_w - own_w, own_w - to_w) & (NZ - 1)
            x_slot, z_slot = lookup(X_ORDER, own_q ^ to_q), lookup(Z_ORDER, step_z)
            index = {
                "x": x_slot * NZ + z_slot,
                "z": (z_slot >> 1) * 2 * NX + x_slot * 2 + (z_slot & 1),
            }
            for k, (axis, start, width, which) in enumerate(PARTS):
                for far in range(2):

                    @pl.when(live & (index[axis] >> 4 == far) & (cluster == which))
                    def _():
                        outs[2 * k + far][index[axis] & 15] += value_ref[
                            t, :, start : start + width
                        ]


def in_hbm(value):
    return pltpu.with_memory_space_constraint(value, pltpu.HBM)


def in_vmem(count):
    return [pl.BlockSpec(memory_space=pltpu.VMEM)] * count


def pin(*values):
    return [pltpu.with_memory_space_constraint(value, pltpu.VMEM) for value in values]


def contributions(block_row, col_count, u_blocks, v_blocks, sketch):
    slots = u_blocks.shape[0]
    shapes = [
        jax.ShapeDtypeStruct((NZ * NX // 2, R, width), jnp.float32)
        for _, _, width, _ in PARTS
        for _ in range(2)
    ]
    return pl.pallas_call(
        contribution_kernel,
        out_shape=shapes,
        in_specs=[pl.BlockSpec(memory_space=pltpu.HBM)] * 5,
        out_specs=in_vmem(len(shapes)),
        scratch_shapes=[
            pltpu.SMEM((slots,), jnp.int32),
            pltpu.SMEM((2,), jnp.int32),
            pltpu.VMEM((slots, R, LEAF), jnp.float32),
            pltpu.VMEM((slots, R, LEAF), jnp.float32),
            pltpu.VMEM((2, R, LEAF), jnp.float32),
            pltpu.VMEM((GROUP, R, LEAF), jnp.float32),
            pltpu.SemaphoreType.DMA((4 + slots // GROUP,)),
        ],
        compiler_params=pltpu.CompilerParams(vmem_limit_bytes=24 << 20),
        cost_estimate=pl.CostEstimate(flops=10**9, bytes_accessed=16 << 20, transcendentals=0),
        name="contributions",
    )(*(in_hbm(a) for a in (block_row, col_count, u_blocks, v_blocks, sketch)))


def exchange(value, axis, step, which):
    pairs = []
    for z in range(NZ):
        for x in range(NX):
            if axis == "x":
                to = z * NX + x_partner(step, which, x)
            else:
                to = z_partner(step, which, z) * NX + x
            pairs.append((z * NX + x, to))
    return lax.ppermute(value, "dev", pairs)


def across(value, step):
    pairs = []
    for g in range(2 * NY):
        y, core = g // 2, g % 2
        to = (g ^ 1, 2 * (y ^ 1) + core, 2 * (y ^ 3) + core)[step]
        pairs.append((g, to))
    return lax.ppermute(value, "grp", pairs)


def scatter_sums(parts):
    kept, last = [], []
    for (first, _, _, which), (keep, send) in zip(PARTS, parts):
        for axis, step in STEPS[first]:
            got = exchange(send, axis, step, which)
            half = keep.shape[0] // 2
            send = keep[half:] + got[half:]
            keep = keep[:half] + got[:half]
        kept.append(keep[0])
        last.append(send)
    terms = []
    for i in range(0, len(PARTS), 2):
        got = exchange(jnp.concatenate(last[i : i + 2], axis=2), "z", 2, PARTS[i][3])
        terms += kept[i : i + 2] + [got[0]]
    return terms


def pack(gram):
    return jnp.concatenate([gram[8 * i : 8 * i + 8] for i in range(4)], axis=1)


def unpack(packed):
    return jnp.concatenate([packed[:, R * i : R * i + R] for i in range(4)], axis=0)


def eliminate(grams):
    eye = (
        lax.broadcasted_iota(jnp.int32, (R, R), 0) == lax.broadcasted_iota(jnp.int32, (R, R), 1)
    ).astype(jnp.float32)
    wide = (R, 2 * R)
    work = [jnp.concatenate([gram, eye], axis=1) for gram in grams]
    done = [[] for _ in grams]
    for first in range(0, R, BLOCK):
        columns = [
            [jnp.broadcast_to(w[:, j : j + 1], wide) for j in range(first, first + BLOCK)]
            for w in work
        ]
        for j in range(first, first + BLOCK):
            for i in range(len(grams)):
                column = columns[i][j - first]
                pivot = column[j : j + 1]
                scale = lax.rsqrt(pivot)
                scale = scale * (1.5 - 0.5 * pivot * scale * scale)
                row = work[i][j : j + 1] * scale
                done[i].append(row)
                factor = column * jnp.broadcast_to(scale, wide)
                for k in range(j + 1, first + BLOCK):
                    entry = columns[i][k - first]
                    columns[i][k - first] = entry - factor * jnp.broadcast_to(
                        entry[j : j + 1] * scale, wide
                    )
                work[i] = work[i] - factor * jnp.broadcast_to(row, wide)
    whole = [jnp.concatenate(rows, axis=0) for rows in done]
    return [(d[:, :R], d[:, R:]) for d in whole]


def sample_kernel(*refs):
    terms, (diag_ref, sketch_ref, sample_ref, gram_ref, packed_ref) = refs[:-5], refs[-5:]
    for k, (_, start, width, which) in enumerate(PARTS):
        columns = slice(start, start + width)
        far = terms[k // 2 * 3 + k % 2][...] + terms[k // 2 * 3 + 2][:, columns]
        near = diag_ref[which : which + 1, columns] * sketch_ref[which, :, columns]
        sample_ref[which, :, columns] = far + near
    total = jnp.zeros((R, R), jnp.float32)
    for i in range(2):
        sample = sample_ref[i]
        gram = lax.dot_general(
            sample,
            sample,
            (((1,), (1,)), ((), ())),
            precision=HIGHEST,
            preferred_element_type=jnp.float32,
        )
        gram_ref[i] = gram
        total = total + gram
    packed_ref[...] = jnp.broadcast_to(pack(total)[None], packed_ref.shape)


def leaf_kernel(gram_ref, sample_ref, basis_ref, upper_ref):
    factors = eliminate([gram_ref[0], gram_ref[1]])
    for i, (upper, inverse) in enumerate(factors):
        upper_ref[i] = upper_part(upper)
        basis_ref[i] = jnp.dot(
            inverse * math.sqrt(LEAF),
            sample_ref[i],
            precision=HIGHEST,
            preferred_element_type=jnp.float32,
        )


def group_kernel(every_ref, packed_ref):
    packed_ref[...] = jnp.sum(every_ref[...], axis=0)


def upper_part(square):
    rows = lax.broadcasted_iota(jnp.int32, (R, R), 0)
    cols = lax.broadcasted_iota(jnp.int32, (R, R), 1)
    return jnp.where(rows <= cols, square, 0.0)


def right_solve(upper, inverse):
    return lax.dot_general(
        upper,
        inverse,
        (((1,), (1,)), ((), ())),
        precision=HIGHEST,
        preferred_element_type=jnp.float32,
    )


def transfer_leaf_kernel(leaves, own_ref, upper_ref, leaf_ref, group_ref):
    ((group_upper, group_inverse),) = eliminate([unpack(own_ref[...])])
    for i in range(2):
        leaf_ref[i] = right_solve(upper_ref[i], group_inverse * math.sqrt(leaves))
    group_ref[...] = upper_part(group_upper)


def transfer_group_kernel(groups, near_ref, far_ref, upper_ref, out_ref):
    ((_, root_inverse),) = eliminate([unpack(near_ref[...] + far_ref[...])])
    out_ref[0] = right_solve(upper_ref[...], root_inverse * math.sqrt(groups))


def body(u_blocks, v_blocks, sketch, near_diag, block_row, col_count):
    members = lax.axis_size("dev")
    groups = lax.axis_size("grp")
    halved = contributions(block_row, col_count, u_blocks, v_blocks, sketch)
    terms = scatter_sums(list(zip(halved[::2], halved[1::2])))
    sample, gram, packed = pl.pallas_call(
        sample_kernel,
        out_shape=(
            pltpu.VMEM((2, R, LEAF), jnp.float32),
            pltpu.VMEM((2, R, R), jnp.float32),
            jax.ShapeDtypeStruct((members, 8, 128), jnp.float32),
        ),
        in_specs=in_vmem(len(terms) + 2),
        out_specs=in_vmem(3),
        name="sample",
    )(*pin(*terms, near_diag, sketch))
    every = lax.all_to_all(packed, "dev", split_axis=0, concat_axis=0, tiled=True)
    leaf_basis, upper = pl.pallas_call(
        leaf_kernel,
        out_shape=(
            jax.ShapeDtypeStruct((2, R, LEAF), jnp.float32),
            pltpu.VMEM((2, R, R), jnp.float32),
        ),
        in_specs=in_vmem(2),
        out_specs=[pl.BlockSpec((2, R, LEAF), lambda: (0, 0, 0))] + in_vmem(1),
        name="leaf",
    )(*pin(gram, sample))
    every, upper = lax.optimization_barrier((every, upper))
    own_gram = pl.pallas_call(
        group_kernel,
        out_shape=pltpu.VMEM((8, 128), jnp.float32),
        in_specs=in_vmem(1),
        out_specs=pl.BlockSpec(memory_space=pltpu.VMEM),
        name="group",
    )(*pin(every))
    total, got = own_gram, across(own_gram, 0)
    for step in range(1, 3):
        total = total + got
        got = across(total, step)
    transfer_leaf, group_upper = pl.pallas_call(
        functools.partial(transfer_leaf_kernel, 2 * members),
        out_shape=(
            jax.ShapeDtypeStruct((2, R, R), jnp.float32),
            pltpu.VMEM((R, R), jnp.float32),
        ),
        in_specs=in_vmem(2),
        name="transfer_leaf",
    )(*pin(own_gram, upper))
    transfer_group = pl.pallas_call(
        functools.partial(transfer_group_kernel, groups),
        out_shape=jax.ShapeDtypeStruct((1, R, R), jnp.float32),
        in_specs=in_vmem(3),
        name="transfer_group",
    )(*pin(total, got, group_upper))
    return (leaf_basis, transfer_leaf, transfer_group)


def solution(mesh):
    in_specs = (
        P(("grp", "dev"), None, None),
        P(("grp", "dev"), None, None),
        P(("grp", "dev"), None, None),
        P(("grp", "dev"), None),
        P(("grp", "dev")),
        P(("grp", "dev")),
    )
    out_specs = (P(("grp", "dev"), None, None), P(("grp", "dev"), None, None), P("grp", None, None))
    return jax.shard_map(body, mesh=mesh, in_specs=in_specs, out_specs=out_specs, check_vma=False)
```

```python
import functools
import math

import jax
import jax.numpy as jnp
from jax import lax
from jax.experimental import pallas as pl
from jax.experimental.pallas import tpu as pltpu
from jax.sharding import PartitionSpec as P

NZ, NX = 8, 4
NY = 4
R = 32
LEAF = 1024
PARTS = (("x", 0, 512, 0), ("z", 512, 512, 0), ("x", 0, 512, 1), ("z", 512, 512, 1))
STEPS = {
    "x": (("x", 0), ("x", 1), ("z", 0), ("z", 1)),
    "z": (("z", 0), ("z", 1), ("x", 0), ("x", 1)),
}
BLOCK = 16
GROUP = 24
HIGHEST = lax.Precision.HIGHEST
X_ORDER, Z_ORDER = (0, 2, 3, 1), (0, 4, 6, 1, 3, 7, 5, 2)


def halves(value):
    high = value.astype(jnp.bfloat16)
    low = (value - high.astype(jnp.float32)).astype(jnp.bfloat16)
    return high, low


def lookup(table, index):
    packed = sum(entry << (4 * i) for i, entry in enumerate(table))
    return (jnp.int32(packed) >> (4 * index)) & 15


def x_partner(step, which, x):
    q = (x - which) % NX
    return ((q ^ 1 if step == 0 else q ^ 3) + which) % NX


def z_partner(step, which, z):
    w = (z - 1 + which) % NZ
    odd = w % 2
    other = (w ^ 1, w - 1 + 2 * odd, w + 3 + 2 * odd)[step]
    return (other + 1 - which) % NZ


def contribution_kernel(rows_hbm, count_hbm, u_hbm, v_hbm, sketch_hbm, *refs):
    outs, scratch = refs[: 2 * len(PARTS)], refs[2 * len(PARTS) :]
    rows_ref, count_ref, u_ref, v_ref, sketch_ref, value_ref, sems = scratch
    slots = u_ref.shape[0]
    groups = slots // GROUP
    small = [
        pltpu.make_async_copy(rows_hbm, rows_ref, sems.at[0]),
        pltpu.make_async_copy(count_hbm, count_ref, sems.at[1]),
        pltpu.make_async_copy(sketch_hbm, sketch_ref, sems.at[2]),
    ]
    large = [pltpu.make_async_copy(v_hbm, v_ref, sems.at[3])] + [
        pltpu.make_async_copy(
            u_hbm.at[pl.ds(g * GROUP, GROUP)], u_ref.at[pl.ds(g * GROUP, GROUP)], sems.at[4 + g]
        )
        for g in range(groups)
    ]
    for copy in small + large:
        copy.start()
    for ref in outs:
        ref[...] = jnp.zeros_like(ref)
    me = lax.axis_index("dev")
    for copy in small:
        copy.wait()
    first_count = count_ref[0]
    live_count = first_count + count_ref[1]
    sketch_high, sketch_low = halves(sketch_ref[...].reshape(2 * R, LEAF))
    both = jnp.concatenate([sketch_high, sketch_low], axis=0)
    contract = (((1,), (1,)), ((), ()))
    large[0].wait()
    v_high, v_low = halves(v_ref[...].reshape(slots * R, LEAF))
    wide = lax.dot_general(v_high, both, contract, preferred_element_type=jnp.float32)
    couplings = (
        wide[:, : 2 * R]
        + wide[:, 2 * R :]
        + lax.dot_general(v_low, sketch_high, contract, preferred_element_type=jnp.float32)
    )
    for g in range(groups):
        large[1 + g].wait()
        for t in range(GROUP):
            part = couplings[(g * GROUP + t) * R : (g * GROUP + t + 1) * R]
            coupling = jnp.where(g * GROUP + t < first_count, part[:, :R], part[:, R:])
            c_high, c_low = halves(coupling)
            u_high, u_low = halves(u_ref[g * GROUP + t])
            left = jnp.concatenate([c_high, c_low, c_high], axis=0)
            right = jnp.concatenate([u_high, u_high, u_low], axis=0)
            value_ref[t] = lax.dot_general(
                left, right, (((0,), (0,)), ((), ())), preferred_element_type=jnp.float32
            )
        for t in range(GROUP):
            slot = g * GROUP + t
            row = rows_ref[slot] & (2 * NZ * NX - 1)
            cluster = row & 1
            live = slot < live_count
            own_w = (me // NX - 1 + cluster) & (NZ - 1)
            own_q = (me % NX - cluster) & (NX - 1)
            to_w = ((row >> 3) - 1 + cluster) & (NZ - 1)
            to_q = (((row >> 1) & (NX - 1)) - cluster) & (NX - 1)
            step_z = jnp.where(own_w & 1 == 0, to_w - own_w, own_w - to_w) & (NZ - 1)
            x_slot, z_slot = lookup(X_ORDER, own_q ^ to_q), lookup(Z_ORDER, step_z)
            index = {
                "x": x_slot * NZ + z_slot,
                "z": (z_slot >> 1) * 2 * NX + x_slot * 2 + (z_slot & 1),
            }
            for k, (axis, start, width, which) in enumerate(PARTS):
                for far in range(2):

                    @pl.when(live & (index[axis] >> 4 == far) & (cluster == which))
                    def _():
                        outs[2 * k + far][index[axis] & 15] += value_ref[
                            t, :, start : start + width
                        ]


def in_hbm(value):
    return pltpu.with_memory_space_constraint(value, pltpu.HBM)


def in_vmem(count):
    return [pl.BlockSpec(memory_space=pltpu.VMEM)] * count


def pin(*values):
    return [pltpu.with_memory_space_constraint(value, pltpu.VMEM) for value in values]


def contributions(block_row, col_count, u_blocks, v_blocks, sketch):
    slots = u_blocks.shape[0]
    shapes = [
        jax.ShapeDtypeStruct((NZ * NX // 2, R, width), jnp.float32)
        for _, _, width, _ in PARTS
        for _ in range(2)
    ]
    return pl.pallas_call(
        contribution_kernel,
        out_shape=shapes,
        in_specs=[pl.BlockSpec(memory_space=pltpu.HBM)] * 5,
        out_specs=in_vmem(len(shapes)),
        scratch_shapes=[
            pltpu.SMEM((slots,), jnp.int32),
            pltpu.SMEM((2,), jnp.int32),
            pltpu.VMEM((slots, R, LEAF), jnp.float32),
            pltpu.VMEM((slots, R, LEAF), jnp.float32),
            pltpu.VMEM((2, R, LEAF), jnp.float32),
            pltpu.VMEM((GROUP, R, LEAF), jnp.float32),
            pltpu.SemaphoreType.DMA((4 + slots // GROUP,)),
        ],
        compiler_params=pltpu.CompilerParams(vmem_limit_bytes=24 << 20),
        cost_estimate=pl.CostEstimate(flops=10**9, bytes_accessed=16 << 20, transcendentals=0),
        name="contributions",
    )(*(in_hbm(a) for a in (block_row, col_count, u_blocks, v_blocks, sketch)))


def exchange(value, axis, step, which):
    pairs = []
    for z in range(NZ):
        for x in range(NX):
            if axis == "x":
                to = z * NX + x_partner(step, which, x)
            else:
                to = z_partner(step, which, z) * NX + x
            pairs.append((z * NX + x, to))
    return lax.ppermute(value, "dev", pairs)


def across(value, step):
    pairs = []
    for g in range(2 * NY):
        y, core = g // 2, g % 2
        to = (g ^ 1, 2 * (y ^ 1) + core, 2 * (y ^ 3) + core)[step]
        pairs.append((g, to))
    return lax.ppermute(value, "grp", pairs)


def scatter_sums(parts):
    kept, last = [], []
    for (first, _, _, which), (keep, send) in zip(PARTS, parts):
        for axis, step in STEPS[first]:
            got = exchange(send, axis, step, which)
            half = keep.shape[0] // 2
            send = keep[half:] + got[half:]
            keep = keep[:half] + got[:half]
        kept.append(keep[0])
        last.append(send)
    terms = []
    for i in range(0, len(PARTS), 2):
        got = exchange(jnp.concatenate(last[i : i + 2], axis=2), "z", 2, PARTS[i][3])
        terms += kept[i : i + 2] + [got[0]]
    return terms


def pack(gram):
    return jnp.concatenate([gram[8 * i : 8 * i + 8] for i in range(4)], axis=1)


def unpack(packed):
    return jnp.concatenate([packed[:, R * i : R * i + R] for i in range(4)], axis=0)


def eliminate(grams):
    eye = (
        lax.broadcasted_iota(jnp.int32, (R, R), 0) == lax.broadcasted_iota(jnp.int32, (R, R), 1)
    ).astype(jnp.float32)
    wide = (R, 2 * R)
    work = [jnp.concatenate([gram, eye], axis=1) for gram in grams]
    done = [[] for _ in grams]
    for first in range(0, R, BLOCK):
        columns = [
            [jnp.broadcast_to(w[:, j : j + 1], wide) for j in range(first, first + BLOCK)]
            for w in work
        ]
        for j in range(first, first + BLOCK):
            for i in range(len(grams)):
                column = columns[i][j - first]
                pivot = column[j : j + 1]
                scale = lax.rsqrt(pivot)
                scale = scale * (1.5 - 0.5 * pivot * scale * scale)
                row = work[i][j : j + 1] * scale
                done[i].append(row)
                factor = column * jnp.broadcast_to(scale, wide)
                for k in range(j + 1, first + BLOCK):
                    entry = columns[i][k - first]
                    columns[i][k - first] = entry - factor * jnp.broadcast_to(
                        entry[j : j + 1] * scale, wide
                    )
                work[i] = work[i] - factor * jnp.broadcast_to(row, wide)
    whole = [jnp.concatenate(rows, axis=0) for rows in done]
    return [(d[:, :R], d[:, R:]) for d in whole]


def sample_kernel(*refs):
    terms, (diag_ref, sketch_ref, sample_ref, gram_ref, packed_ref) = refs[:-5], refs[-5:]
    for k, (_, start, width, which) in enumerate(PARTS):
        columns = slice(start, start + width)
        far = terms[k // 2 * 3 + k % 2][...] + terms[k // 2 * 3 + 2][:, columns]
        near = diag_ref[which : which + 1, columns] * sketch_ref[which, :, columns]
        sample_ref[which, :, columns] = far + near
    total = jnp.zeros((R, R), jnp.float32)
    for i in range(2):
        sample = sample_ref[i]
        gram = lax.dot_general(
            sample,
            sample,
            (((1,), (1,)), ((), ())),
            precision=HIGHEST,
            preferred_element_type=jnp.float32,
        )
        gram_ref[i] = gram
        total = total + gram
    packed_ref[...] = jnp.broadcast_to(pack(total)[None], packed_ref.shape)


def leaf_kernel(gram_ref, sample_ref, basis_ref, upper_ref):
    factors = eliminate([gram_ref[0], gram_ref[1]])
    for i, (upper, inverse) in enumerate(factors):
        upper_ref[i] = upper_part(upper)
        basis_ref[i] = jnp.dot(
            inverse * math.sqrt(LEAF),
            sample_ref[i],
            precision=HIGHEST,
            preferred_element_type=jnp.float32,
        )


def group_kernel(every_ref, packed_ref):
    packed_ref[...] = jnp.sum(every_ref[...], axis=0)


def upper_part(square):
    rows = lax.broadcasted_iota(jnp.int32, (R, R), 0)
    cols = lax.broadcasted_iota(jnp.int32, (R, R), 1)
    return jnp.where(rows <= cols, square, 0.0)


def right_solve(upper, inverse):
    return lax.dot_general(
        upper,
        inverse,
        (((1,), (1,)), ((), ())),
        precision=HIGHEST,
        preferred_element_type=jnp.float32,
    )


def transfer_leaf_kernel(leaves, own_ref, upper_ref, leaf_ref, group_ref):
    ((group_upper, group_inverse),) = eliminate([unpack(own_ref[...])])
    for i in range(2):
        leaf_ref[i] = right_solve(upper_ref[i], group_inverse * math.sqrt(leaves))
    group_ref[...] = upper_part(group_upper)


def transfer_group_kernel(groups, near_ref, far_ref, upper_ref, out_ref):
    ((_, root_inverse),) = eliminate([unpack(near_ref[...] + far_ref[...])])
    out_ref[0] = right_solve(upper_ref[...], root_inverse * math.sqrt(groups))


def body(u_blocks, v_blocks, sketch, near_diag, block_row, col_count):
    members = lax.axis_size("dev")
    groups = lax.axis_size("grp")
    halved = contributions(block_row, col_count, u_blocks, v_blocks, sketch)
    terms = scatter_sums(list(zip(halved[::2], halved[1::2])))
    sample, gram, packed = pl.pallas_call(
        sample_kernel,
        out_shape=(
            pltpu.VMEM((2, R, LEAF), jnp.float32),
            pltpu.VMEM((2, R, R), jnp.float32),
            pltpu.VMEM((members, 8, 128), jnp.float32),
        ),
        in_specs=in_vmem(len(terms) + 2),
        out_specs=in_vmem(3),
        name="sample",
    )(*pin(*terms, near_diag, sketch))
    every = lax.all_to_all(packed, "dev", split_axis=0, concat_axis=0, tiled=True)
    leaf_basis, upper = pl.pallas_call(
        leaf_kernel,
        out_shape=(
            jax.ShapeDtypeStruct((2, R, LEAF), jnp.float32),
            pltpu.VMEM((2, R, R), jnp.float32),
        ),
        in_specs=in_vmem(2),
        out_specs=[pl.BlockSpec((2, R, LEAF), lambda: (0, 0, 0))] + in_vmem(1),
        name="leaf",
    )(*pin(gram, sample))
    every, upper = lax.optimization_barrier((every, upper))
    own_gram = pl.pallas_call(
        group_kernel,
        out_shape=pltpu.VMEM((8, 128), jnp.float32),
        in_specs=in_vmem(1),
        out_specs=pl.BlockSpec(memory_space=pltpu.VMEM),
        name="group",
    )(*pin(every))
    total, got = own_gram, across(own_gram, 0)
    for step in range(1, 3):
        total = total + got
        got = across(total, step)
    transfer_leaf, group_upper = pl.pallas_call(
        functools.partial(transfer_leaf_kernel, 2 * members),
        out_shape=(
            jax.ShapeDtypeStruct((2, R, R), jnp.float32),
            pltpu.VMEM((R, R), jnp.float32),
        ),
        in_specs=in_vmem(2),
        name="transfer_leaf",
    )(*pin(own_gram, upper))
    transfer_group = pl.pallas_call(
        functools.partial(transfer_group_kernel, groups),
        out_shape=jax.ShapeDtypeStruct((1, R, R), jnp.float32),
        in_specs=in_vmem(3),
        name="transfer_group",
    )(*pin(total, got, group_upper))
    return (leaf_basis, transfer_leaf, transfer_group)


def solution(mesh):
    in_specs = (
        P(("grp", "dev"), None, None),
        P(("grp", "dev"), None, None),
        P(("grp", "dev"), None, None),
        P(("grp", "dev"), None),
        P(("grp", "dev")),
        P(("grp", "dev")),
    )
    out_specs = (P(("grp", "dev"), None, None), P(("grp", "dev"), None, None), P("grp", None, None))
    return jax.shard_map(body, mesh=mesh, in_specs=in_specs, out_specs=out_specs, check_vma=False)
```

```python
import functools
import math

import jax
import jax.numpy as jnp
from jax import lax
from jax.experimental import pallas as pl
from jax.experimental.pallas import tpu as pltpu
from jax.sharding import PartitionSpec as P

NZ, NX = 8, 4
NY = 4
R = 32
LEAF = 1024
PARTS = (("x", 0, 512, 0), ("z", 512, 512, 0), ("z", 512, 512, 1), ("x", 0, 512, 1))
STEPS = {
    "x": (("x", 0), ("x", 1), ("z", 0), ("z", 1)),
    "z": (("z", 0), ("z", 1), ("x", 0), ("x", 1)),
}
BLOCK = 16
GROUP = 24
HIGHEST = lax.Precision.HIGHEST
X_ORDER, Z_ORDER = (0, 2, 3, 1), (0, 4, 6, 1, 3, 7, 5, 2)


def halves(value):
    high = value.astype(jnp.bfloat16)
    low = (value - high.astype(jnp.float32)).astype(jnp.bfloat16)
    return high, low


def lookup(table, index):
    packed = sum(entry << (4 * i) for i, entry in enumerate(table))
    return (jnp.int32(packed) >> (4 * index)) & 15


def x_partner(step, which, x):
    q = (x - which) % NX
    return ((q ^ 1 if step == 0 else q ^ 3) + which) % NX


def z_partner(step, which, z):
    w = (z - 1 + which) % NZ
    odd = w % 2
    other = (w ^ 1, w - 1 + 2 * odd, w + 3 + 2 * odd)[step]
    return (other + 1 - which) % NZ


def contribution_kernel(rows_hbm, count_hbm, u_hbm, v_hbm, sketch_hbm, *refs):
    outs, scratch = refs[: 2 * len(PARTS)], refs[2 * len(PARTS) :]
    rows_ref, count_ref, u_ref, v_ref, sketch_ref, value_ref, sems = scratch
    slots = u_ref.shape[0]
    groups = slots // GROUP
    small = [
        pltpu.make_async_copy(rows_hbm, rows_ref, sems.at[0]),
        pltpu.make_async_copy(count_hbm, count_ref, sems.at[1]),
        pltpu.make_async_copy(sketch_hbm, sketch_ref, sems.at[2]),
    ]
    large = [pltpu.make_async_copy(v_hbm, v_ref, sems.at[3])] + [
        pltpu.make_async_copy(
            u_hbm.at[pl.ds(g * GROUP, GROUP)], u_ref.at[pl.ds(g * GROUP, GROUP)], sems.at[4 + g]
        )
        for g in range(groups)
    ]
    for copy in small + large:
        copy.start()
    for ref in outs:
        ref[...] = jnp.zeros_like(ref)
    me = lax.axis_index("dev")
    for copy in small:
        copy.wait()
    first_count = count_ref[0]
    live_count = first_count + count_ref[1]
    sketch_high, sketch_low = halves(sketch_ref[...].reshape(2 * R, LEAF))
    both = jnp.concatenate([sketch_high, sketch_low], axis=0)
    contract = (((1,), (1,)), ((), ()))
    large[0].wait()
    v_high, v_low = halves(v_ref[...].reshape(slots * R, LEAF))
    wide = lax.dot_general(v_high, both, contract, preferred_element_type=jnp.float32)
    couplings = (
        wide[:, : 2 * R]
        + wide[:, 2 * R :]
        + lax.dot_general(v_low, sketch_high, contract, preferred_element_type=jnp.float32)
    )
    for g in range(groups):
        large[1 + g].wait()
        for t in range(GROUP):
            part = couplings[(g * GROUP + t) * R : (g * GROUP + t + 1) * R]
            coupling = jnp.where(g * GROUP + t < first_count, part[:, :R], part[:, R:])
            c_high, c_low = halves(coupling)
            u_high, u_low = halves(u_ref[g * GROUP + t])
            left = jnp.concatenate([c_high, c_low, c_high], axis=0)
            right = jnp.concatenate([u_high, u_high, u_low], axis=0)
            value_ref[t] = lax.dot_general(
                left, right, (((0,), (0,)), ((), ())), preferred_element_type=jnp.float32
            )
        for t in range(GROUP):
            slot = g * GROUP + t
            row = rows_ref[slot] & (2 * NZ * NX - 1)
            cluster = row & 1
            live = slot < live_count
            own_w = (me // NX - 1 + cluster) & (NZ - 1)
            own_q = (me % NX - cluster) & (NX - 1)
            to_w = ((row >> 3) - 1 + cluster) & (NZ - 1)
            to_q = (((row >> 1) & (NX - 1)) - cluster) & (NX - 1)
            step_z = jnp.where(own_w & 1 == 0, to_w - own_w, own_w - to_w) & (NZ - 1)
            x_slot, z_slot = lookup(X_ORDER, own_q ^ to_q), lookup(Z_ORDER, step_z)
            index = {
                "x": x_slot * NZ + z_slot,
                "z": (z_slot >> 1) * 2 * NX + x_slot * 2 + (z_slot & 1),
            }
            for k, (axis, start, width, which) in enumerate(PARTS):
                for far in range(2):

                    @pl.when(live & (index[axis] >> 4 == far) & (cluster == which))
                    def _():
                        outs[2 * k + far][index[axis] & 15] += value_ref[
                            t, :, start : start + width
                        ]


def in_hbm(value):
    return pltpu.with_memory_space_constraint(value, pltpu.HBM)


def in_vmem(count):
    return [pl.BlockSpec(memory_space=pltpu.VMEM)] * count


def pin(*values):
    return [pltpu.with_memory_space_constraint(value, pltpu.VMEM) for value in values]


def contributions(block_row, col_count, u_blocks, v_blocks, sketch):
    slots = u_blocks.shape[0]
    shapes = [
        jax.ShapeDtypeStruct((NZ * NX // 2, R, width), jnp.float32)
        for _, _, width, _ in PARTS
        for _ in range(2)
    ]
    return pl.pallas_call(
        contribution_kernel,
        out_shape=shapes,
        in_specs=[pl.BlockSpec(memory_space=pltpu.HBM)] * 5,
        out_specs=in_vmem(len(shapes)),
        scratch_shapes=[
            pltpu.SMEM((slots,), jnp.int32),
            pltpu.SMEM((2,), jnp.int32),
            pltpu.VMEM((slots, R, LEAF), jnp.float32),
            pltpu.VMEM((slots, R, LEAF), jnp.float32),
            pltpu.VMEM((2, R, LEAF), jnp.float32),
            pltpu.VMEM((GROUP, R, LEAF), jnp.float32),
            pltpu.SemaphoreType.DMA((4 + slots // GROUP,)),
        ],
        compiler_params=pltpu.CompilerParams(vmem_limit_bytes=24 << 20),
        cost_estimate=pl.CostEstimate(flops=10**9, bytes_accessed=16 << 20, transcendentals=0),
        name="contributions",
    )(*(in_hbm(a) for a in (block_row, col_count, u_blocks, v_blocks, sketch)))


def exchange(value, axis, step, which):
    pairs = []
    for z in range(NZ):
        for x in range(NX):
            if axis == "x":
                to = z * NX + x_partner(step, which, x)
            else:
                to = z_partner(step, which, z) * NX + x
            pairs.append((z * NX + x, to))
    return lax.ppermute(value, "dev", pairs)


def across(value, step):
    pairs = []
    for g in range(2 * NY):
        y, core = g // 2, g % 2
        to = (g ^ 1, 2 * (y ^ 3) + core, 2 * (y ^ 1) + core)[step]
        pairs.append((g, to))
    return lax.ppermute(value, "grp", pairs)


def scatter_sums(parts):
    kept, last = {}, {}
    for (first, _, _, which), (keep, send) in zip(PARTS, parts):
        for axis, step in STEPS[first]:
            got = exchange(send, axis, step, which)
            half = keep.shape[0] // 2
            send = keep[half:] + got[half:]
            keep = keep[:half] + got[:half]
        kept[first, which], last[first, which] = keep[0], send
    terms = []
    for which in range(2):
        got = exchange(jnp.concatenate([last["x", which], last["z", which]], axis=2), "z", 2, which)
        terms += [kept["x", which], kept["z", which], got[0]]
    return terms


def pack(gram):
    return jnp.concatenate([gram[8 * i : 8 * i + 8] for i in range(4)], axis=1)


def unpack(packed):
    return jnp.concatenate([packed[:, R * i : R * i + R] for i in range(4)], axis=0)


def eliminate(grams):
    eye = (
        lax.broadcasted_iota(jnp.int32, (R, R), 0) == lax.broadcasted_iota(jnp.int32, (R, R), 1)
    ).astype(jnp.float32)
    wide = (R, 2 * R)
    work = [jnp.concatenate([gram, eye], axis=1) for gram in grams]
    done = [[] for _ in grams]
    for first in range(0, R, BLOCK):
        columns = [
            [jnp.broadcast_to(w[:, j : j + 1], wide) for j in range(first, first + BLOCK)]
            for w in work
        ]
        for j in range(first, first + BLOCK):
            for i in range(len(grams)):
                column = columns[i][j - first]
                pivot = column[j : j + 1]
                scale = lax.rsqrt(pivot)
                scale = scale * (1.5 - 0.5 * pivot * scale * scale)
                row = work[i][j : j + 1] * scale
                done[i].append(row)
                factor = column * jnp.broadcast_to(scale, wide)
                for k in range(j + 1, first + BLOCK):
                    entry = columns[i][k - first]
                    columns[i][k - first] = entry - factor * jnp.broadcast_to(
                        entry[j : j + 1] * scale, wide
                    )
                work[i] = work[i] - factor * jnp.broadcast_to(row, wide)
    whole = [jnp.concatenate(rows, axis=0) for rows in done]
    return [(d[:, :R], d[:, R:]) for d in whole]


def sample_kernel(*refs):
    terms, (diag_ref, sketch_ref, sample_ref, gram_ref, packed_ref) = refs[:-5], refs[-5:]
    for first, start, width, which in PARTS:
        columns = slice(start, start + width)
        far = terms[3 * which + (first == "z")][...] + terms[3 * which + 2][:, columns]
        near = diag_ref[which : which + 1, columns] * sketch_ref[which, :, columns]
        sample_ref[which, :, columns] = far + near
    total = jnp.zeros((R, R), jnp.float32)
    for i in range(2):
        sample = sample_ref[i]
        gram = lax.dot_general(
            sample,
            sample,
            (((1,), (1,)), ((), ())),
            precision=HIGHEST,
            preferred_element_type=jnp.float32,
        )
        gram_ref[i] = gram
        total = total + gram
    packed_ref[...] = jnp.broadcast_to(pack(total)[None], packed_ref.shape)


def leaf_kernel(gram_ref, sample_ref, basis_ref, upper_ref):
    factors = eliminate([gram_ref[0], gram_ref[1]])
    for i, (upper, inverse) in enumerate(factors):
        upper_ref[i] = upper_part(upper)
        basis_ref[i] = jnp.dot(
            inverse * math.sqrt(LEAF),
            sample_ref[i],
            precision=HIGHEST,
            preferred_element_type=jnp.float32,
        )


def group_kernel(every_ref, packed_ref):
    packed_ref[...] = jnp.sum(every_ref[...], axis=0)


def upper_part(square):
    rows = lax.broadcasted_iota(jnp.int32, (R, R), 0)
    cols = lax.broadcasted_iota(jnp.int32, (R, R), 1)
    return jnp.where(rows <= cols, square, 0.0)


def right_solve(upper, inverse):
    return lax.dot_general(
        upper,
        inverse,
        (((1,), (1,)), ((), ())),
        precision=HIGHEST,
        preferred_element_type=jnp.float32,
    )


def transfer_leaf_kernel(leaves, own_ref, upper_ref, leaf_ref, group_ref):
    ((group_upper, group_inverse),) = eliminate([unpack(own_ref[...])])
    for i in range(2):
        leaf_ref[i] = right_solve(upper_ref[i], group_inverse * math.sqrt(leaves))
    group_ref[...] = upper_part(group_upper)


def transfer_group_kernel(groups, near_ref, far_ref, upper_ref, out_ref):
    ((_, root_inverse),) = eliminate([unpack(near_ref[...] + far_ref[...])])
    out_ref[0] = right_solve(upper_ref[...], root_inverse * math.sqrt(groups))


def body(u_blocks, v_blocks, sketch, near_diag, block_row, col_count):
    members = lax.axis_size("dev")
    groups = lax.axis_size("grp")
    halved = contributions(block_row, col_count, u_blocks, v_blocks, sketch)
    terms = scatter_sums(list(zip(halved[::2], halved[1::2])))
    sample, gram, packed = pl.pallas_call(
        sample_kernel,
        out_shape=(
            pltpu.VMEM((2, R, LEAF), jnp.float32),
            pltpu.VMEM((2, R, R), jnp.float32),
            pltpu.VMEM((members, 8, 128), jnp.float32),
        ),
        in_specs=in_vmem(len(terms) + 2),
        out_specs=in_vmem(3),
        name="sample",
    )(*pin(*terms, near_diag, sketch))
    every = lax.all_to_all(packed, "dev", split_axis=0, concat_axis=0, tiled=True)
    leaf_basis, upper = pl.pallas_call(
        leaf_kernel,
        out_shape=(
            jax.ShapeDtypeStruct((2, R, LEAF), jnp.float32),
            pltpu.VMEM((2, R, R), jnp.float32),
        ),
        in_specs=in_vmem(2),
        out_specs=[pl.BlockSpec((2, R, LEAF), lambda: (0, 0, 0))] + in_vmem(1),
        name="leaf",
    )(*pin(gram, sample))
    every, upper = lax.optimization_barrier((every, upper))
    own_gram = pl.pallas_call(
        group_kernel,
        out_shape=pltpu.VMEM((8, 128), jnp.float32),
        in_specs=in_vmem(1),
        out_specs=pl.BlockSpec(memory_space=pltpu.VMEM),
        name="group",
    )(*pin(every))
    total, got = own_gram, across(own_gram, 0)
    for step in range(1, 3):
        total = total + got
        got = across(total, step)
    transfer_leaf, group_upper = pl.pallas_call(
        functools.partial(transfer_leaf_kernel, 2 * members),
        out_shape=(
            jax.ShapeDtypeStruct((2, R, R), jnp.float32),
            pltpu.VMEM((R, R), jnp.float32),
        ),
        in_specs=in_vmem(2),
        name="transfer_leaf",
    )(*pin(own_gram, upper))
    transfer_group = pl.pallas_call(
        functools.partial(transfer_group_kernel, groups),
        out_shape=jax.ShapeDtypeStruct((1, R, R), jnp.float32),
        in_specs=in_vmem(3),
        name="transfer_group",
    )(*pin(total, got, group_upper))
    return (leaf_basis, transfer_leaf, transfer_group)


def solution(mesh):
    in_specs = (
        P(("grp", "dev"), None, None),
        P(("grp", "dev"), None, None),
        P(("grp", "dev"), None, None),
        P(("grp", "dev"), None),
        P(("grp", "dev")),
        P(("grp", "dev")),
    )
    out_specs = (P(("grp", "dev"), None, None), P(("grp", "dev"), None, None), P("grp", None, None))
    return jax.shard_map(body, mesh=mesh, in_specs=in_specs, out_specs=out_specs, check_vma=False)
```

```python
import functools
import math

import jax
import jax.numpy as jnp
from jax import lax
from jax.experimental import pallas as pl
from jax.experimental.pallas import tpu as pltpu
from jax.sharding import PartitionSpec as P

NZ, NX = 8, 4
NY = 4
R = 32
LEAF = 1024
PARTS = (("x", 0, 512, 0), ("z", 512, 512, 0), ("x", 0, 512, 1), ("z", 512, 512, 1))
STEPS = {
    "x": (("x", 0), ("x", 1), ("z", 0), ("z", 1)),
    "z": (("z", 0), ("z", 1), ("x", 0), ("x", 1)),
}
BLOCK = 16
GROUP = 24
HIGHEST = lax.Precision.HIGHEST
X_ORDER, Z_ORDER = (0, 2, 3, 1), (0, 4, 6, 1, 3, 7, 5, 2)


def halves(value):
    high = value.astype(jnp.bfloat16)
    low = (value - high.astype(jnp.float32)).astype(jnp.bfloat16)
    return high, low


def lookup(table, index):
    packed = sum(entry << (4 * i) for i, entry in enumerate(table))
    return (jnp.int32(packed) >> (4 * index)) & 15


def x_partner(step, which, x):
    q = (x - which) % NX
    return ((q ^ 1 if step == 0 else q ^ 3) + which) % NX


def z_partner(step, which, z):
    w = (z - 1 + which) % NZ
    odd = w % 2
    other = (w ^ 1, w - 1 + 2 * odd, w + 3 + 2 * odd)[step]
    return (other + 1 - which) % NZ


def contribution_kernel(rows_hbm, count_hbm, u_hbm, v_hbm, sketch_hbm, *refs):
    outs, scratch = refs[: 2 * len(PARTS)], refs[2 * len(PARTS) :]
    rows_ref, count_ref, u_ref, v_ref, sketch_ref, value_ref, sems = scratch
    slots = u_ref.shape[0]
    groups = slots // GROUP
    small = [
        pltpu.make_async_copy(rows_hbm, rows_ref, sems.at[0]),
        pltpu.make_async_copy(count_hbm, count_ref, sems.at[1]),
        pltpu.make_async_copy(sketch_hbm, sketch_ref, sems.at[2]),
    ]
    large = [pltpu.make_async_copy(v_hbm, v_ref, sems.at[3])] + [
        pltpu.make_async_copy(
            u_hbm.at[pl.ds(g * GROUP, GROUP)], u_ref.at[pl.ds(g * GROUP, GROUP)], sems.at[4 + g]
        )
        for g in range(groups)
    ]
    for copy in small + large:
        copy.start()
    for ref in outs:
        ref[...] = jnp.zeros_like(ref)
    me = lax.axis_index("dev")
    for copy in small:
        copy.wait()
    first_count = count_ref[0]
    live_count = first_count + count_ref[1]
    sketch_high, sketch_low = halves(sketch_ref[...].reshape(2 * R, LEAF))
    both = jnp.concatenate([sketch_high, sketch_low], axis=0)
    contract = (((1,), (1,)), ((), ()))
    large[0].wait()
    v_high, v_low = halves(v_ref[...].reshape(slots * R, LEAF))
    wide = lax.dot_general(v_high, both, contract, preferred_element_type=jnp.float32)
    couplings = (
        wide[:, : 2 * R]
        + wide[:, 2 * R :]
        + lax.dot_general(v_low, sketch_high, contract, preferred_element_type=jnp.float32)
    )
    for g in range(groups):
        large[1 + g].wait()
        for t in range(GROUP):
            part = couplings[(g * GROUP + t) * R : (g * GROUP + t + 1) * R]
            coupling = jnp.where(g * GROUP + t < first_count, part[:, :R], part[:, R:])
            c_high, c_low = halves(coupling)
            u_high, u_low = halves(u_ref[g * GROUP + t])
            left = jnp.concatenate([c_high, c_low, c_high], axis=0)
            right = jnp.concatenate([u_high, u_high, u_low], axis=0)
            value_ref[t] = lax.dot_general(
                left, right, (((0,), (0,)), ((), ())), preferred_element_type=jnp.float32
            )
        for t in range(GROUP):
            slot = g * GROUP + t
            row = rows_ref[slot] & (2 * NZ * NX - 1)
            cluster = row & 1
            live = slot < live_count
            own_w = (me // NX - 1 + cluster) & (NZ - 1)
            to_w = ((row >> 3) - 1 + cluster) & (NZ - 1)
            step_z = jnp.where(own_w & 1 == 0, to_w - own_w, own_w - to_w) & (NZ - 1)
            z_slot = lookup(Z_ORDER, step_z)
            x_slot, x_late = (
                lookup(X_ORDER, ((me - colour) & (NX - 1)) ^ (((row >> 1) - colour) & (NX - 1)))
                for colour in (cluster, 1 - cluster)
            )
            index = {
                "x": x_slot * NZ + z_slot,
                "z": (z_slot >> 1) * 2 * NX + x_late * 2 + (z_slot & 1),
            }
            for k, (axis, start, width, which) in enumerate(PARTS):
                for far in range(2):

                    @pl.when(live & (index[axis] >> 4 == far) & (cluster == which))
                    def _():
                        outs[2 * k + far][index[axis] & 15] += value_ref[
                            t, :, start : start + width
                        ]


def in_hbm(value):
    return pltpu.with_memory_space_constraint(value, pltpu.HBM)


def in_vmem(count):
    return [pl.BlockSpec(memory_space=pltpu.VMEM)] * count


def pin(*values):
    return [pltpu.with_memory_space_constraint(value, pltpu.VMEM) for value in values]


def contributions(block_row, col_count, u_blocks, v_blocks, sketch):
    slots = u_blocks.shape[0]
    shapes = [
        jax.ShapeDtypeStruct((NZ * NX // 2, R, width), jnp.float32)
        for _, _, width, _ in PARTS
        for _ in range(2)
    ]
    return pl.pallas_call(
        contribution_kernel,
        out_shape=shapes,
        in_specs=[pl.BlockSpec(memory_space=pltpu.HBM)] * 5,
        out_specs=in_vmem(len(shapes)),
        scratch_shapes=[
            pltpu.SMEM((slots,), jnp.int32),
            pltpu.SMEM((2,), jnp.int32),
            pltpu.VMEM((slots, R, LEAF), jnp.float32),
            pltpu.VMEM((slots, R, LEAF), jnp.float32),
            pltpu.VMEM((2, R, LEAF), jnp.float32),
            pltpu.VMEM((GROUP, R, LEAF), jnp.float32),
            pltpu.SemaphoreType.DMA((4 + slots // GROUP,)),
        ],
        compiler_params=pltpu.CompilerParams(vmem_limit_bytes=24 << 20),
        cost_estimate=pl.CostEstimate(flops=10**9, bytes_accessed=16 << 20, transcendentals=0),
        name="contributions",
    )(*(in_hbm(a) for a in (block_row, col_count, u_blocks, v_blocks, sketch)))


def exchange(value, axis, step, which):
    pairs = []
    for z in range(NZ):
        for x in range(NX):
            if axis == "x":
                to = z * NX + x_partner(step, which, x)
            else:
                to = z_partner(step, which, z) * NX + x
            pairs.append((z * NX + x, to))
    return lax.ppermute(value, "dev", pairs)


def across(value, step):
    pairs = []
    for g in range(2 * NY):
        y, core = g // 2, g % 2
        to = (g ^ 1, 2 * (y ^ 1) + core, 2 * (y ^ 3) + core)[step]
        pairs.append((g, to))
    return lax.ppermute(value, "grp", pairs)


def scatter_sums(parts):
    kept, last = [], []
    for (first, _, _, which), (keep, send) in zip(PARTS, parts):
        for axis, step in STEPS[first]:
            late = first == "z" and axis == "x"
            got = exchange(send, axis, step, 1 - which if late else which)
            half = keep.shape[0] // 2
            send = keep[half:] + got[half:]
            keep = keep[:half] + got[:half]
        kept.append(keep[0])
        last.append(send)
    terms = []
    for i in range(0, len(PARTS), 2):
        got = exchange(jnp.concatenate(last[i : i + 2], axis=2), "z", 2, PARTS[i][3])
        terms += kept[i : i + 2] + [got[0]]
    return terms


def pack(gram):
    return jnp.concatenate([gram[8 * i : 8 * i + 8] for i in range(4)], axis=1)


def unpack(packed):
    return jnp.concatenate([packed[:, R * i : R * i + R] for i in range(4)], axis=0)


def eliminate(grams):
    eye = (
        lax.broadcasted_iota(jnp.int32, (R, R), 0) == lax.broadcasted_iota(jnp.int32, (R, R), 1)
    ).astype(jnp.float32)
    wide = (R, 2 * R)
    work = [jnp.concatenate([gram, eye], axis=1) for gram in grams]
    done = [[] for _ in grams]
    for first in range(0, R, BLOCK):
        columns = [
            [jnp.broadcast_to(w[:, j : j + 1], wide) for j in range(first, first + BLOCK)]
            for w in work
        ]
        for j in range(first, first + BLOCK):
            for i in range(len(grams)):
                column = columns[i][j - first]
                pivot = column[j : j + 1]
                scale = lax.rsqrt(pivot)
                scale = scale * (1.5 - 0.5 * pivot * scale * scale)
                row = work[i][j : j + 1] * scale
                done[i].append(row)
                factor = column * jnp.broadcast_to(scale, wide)
                for k in range(j + 1, first + BLOCK):
                    entry = columns[i][k - first]
                    columns[i][k - first] = entry - factor * jnp.broadcast_to(
                        entry[j : j + 1] * scale, wide
                    )
                work[i] = work[i] - factor * jnp.broadcast_to(row, wide)
    whole = [jnp.concatenate(rows, axis=0) for rows in done]
    return [(d[:, :R], d[:, R:]) for d in whole]


def sample_kernel(*refs):
    terms, (diag_ref, sketch_ref, sample_ref, gram_ref, packed_ref) = refs[:-5], refs[-5:]
    for k, (_, start, width, which) in enumerate(PARTS):
        columns = slice(start, start + width)
        far = terms[k // 2 * 3 + k % 2][...] + terms[k // 2 * 3 + 2][:, columns]
        near = diag_ref[which : which + 1, columns] * sketch_ref[which, :, columns]
        sample_ref[which, :, columns] = far + near
    total = jnp.zeros((R, R), jnp.float32)
    for i in range(2):
        sample = sample_ref[i]
        gram = lax.dot_general(
            sample,
            sample,
            (((1,), (1,)), ((), ())),
            precision=HIGHEST,
            preferred_element_type=jnp.float32,
        )
        gram_ref[i] = gram
        total = total + gram
    packed_ref[...] = jnp.broadcast_to(pack(total)[None], packed_ref.shape)


def leaf_kernel(gram_ref, sample_ref, basis_ref, upper_ref):
    factors = eliminate([gram_ref[0], gram_ref[1]])
    for i, (upper, inverse) in enumerate(factors):
        upper_ref[i] = upper_part(upper)
        basis_ref[i] = jnp.dot(
            inverse * math.sqrt(LEAF),
            sample_ref[i],
            precision=HIGHEST,
            preferred_element_type=jnp.float32,
        )


def group_kernel(every_ref, packed_ref):
    packed_ref[...] = jnp.sum(every_ref[...], axis=0)


def upper_part(square):
    rows = lax.broadcasted_iota(jnp.int32, (R, R), 0)
    cols = lax.broadcasted_iota(jnp.int32, (R, R), 1)
    return jnp.where(rows <= cols, square, 0.0)


def right_solve(upper, inverse):
    return lax.dot_general(
        upper,
        inverse,
        (((1,), (1,)), ((), ())),
        precision=HIGHEST,
        preferred_element_type=jnp.float32,
    )


def transfer_leaf_kernel(leaves, own_ref, upper_ref, leaf_ref, group_ref):
    ((group_upper, group_inverse),) = eliminate([unpack(own_ref[...])])
    for i in range(2):
        leaf_ref[i] = right_solve(upper_ref[i], group_inverse * math.sqrt(leaves))
    group_ref[...] = upper_part(group_upper)


def transfer_group_kernel(groups, near_ref, far_ref, upper_ref, out_ref):
    ((_, root_inverse),) = eliminate([unpack(near_ref[...] + far_ref[...])])
    out_ref[0] = right_solve(upper_ref[...], root_inverse * math.sqrt(groups))


def body(u_blocks, v_blocks, sketch, near_diag, block_row, col_count):
    members = lax.axis_size("dev")
    groups = lax.axis_size("grp")
    halved = contributions(block_row, col_count, u_blocks, v_blocks, sketch)
    terms = scatter_sums(list(zip(halved[::2], halved[1::2])))
    sample, gram, packed = pl.pallas_call(
        sample_kernel,
        out_shape=(
            pltpu.VMEM((2, R, LEAF), jnp.float32),
            pltpu.VMEM((2, R, R), jnp.float32),
            pltpu.VMEM((members, 8, 128), jnp.float32),
        ),
        in_specs=in_vmem(len(terms) + 2),
        out_specs=in_vmem(3),
        name="sample",
    )(*pin(*terms, near_diag, sketch))
    every = lax.all_to_all(packed, "dev", split_axis=0, concat_axis=0, tiled=True)
    leaf_basis, upper = pl.pallas_call(
        leaf_kernel,
        out_shape=(
            jax.ShapeDtypeStruct((2, R, LEAF), jnp.float32),
            pltpu.VMEM((2, R, R), jnp.float32),
        ),
        in_specs=in_vmem(2),
        out_specs=[pl.BlockSpec((2, R, LEAF), lambda: (0, 0, 0))] + in_vmem(1),
        name="leaf",
    )(*pin(gram, sample))
    every, upper = lax.optimization_barrier((every, upper))
    own_gram = pl.pallas_call(
        group_kernel,
        out_shape=pltpu.VMEM((8, 128), jnp.float32),
        in_specs=in_vmem(1),
        out_specs=pl.BlockSpec(memory_space=pltpu.VMEM),
        name="group",
    )(*pin(every))
    total, got = own_gram, across(own_gram, 0)
    for step in range(1, 3):
        total = total + got
        got = across(total, step)
    transfer_leaf, group_upper = pl.pallas_call(
        functools.partial(transfer_leaf_kernel, 2 * members),
        out_shape=(
            jax.ShapeDtypeStruct((2, R, R), jnp.float32),
            pltpu.VMEM((R, R), jnp.float32),
        ),
        in_specs=in_vmem(2),
        name="transfer_leaf",
    )(*pin(own_gram, upper))
    transfer_group = pl.pallas_call(
        functools.partial(transfer_group_kernel, groups),
        out_shape=jax.ShapeDtypeStruct((1, R, R), jnp.float32),
        in_specs=in_vmem(3),
        name="transfer_group",
    )(*pin(total, got, group_upper))
    return (leaf_basis, transfer_leaf, transfer_group)


def solution(mesh):
    in_specs = (
        P(("grp", "dev"), None, None),
        P(("grp", "dev"), None, None),
        P(("grp", "dev"), None, None),
        P(("grp", "dev"), None),
        P(("grp", "dev")),
        P(("grp", "dev")),
    )
    out_specs = (P(("grp", "dev"), None, None), P(("grp", "dev"), None, None), P("grp", None, None))
    return jax.shard_map(body, mesh=mesh, in_specs=in_specs, out_specs=out_specs, check_vma=False)
```
